256 devices in a mesh: clip: 16 (over z, core), row: 4 (over y), tm: 4 (over x).
Axes of the slice: x: 4, y: 4, z: 8, core: 2. Of those that a mesh axis runs over, the one named last changes fastest.
Arguments:
- frames: bfloat16 [128, 3, 16, 1024], P('clip', None, 'tm', 'row'), may hold values from -6 to 6
- keep_list: int32 [128], P('clip'), may hold values from -1 to 63, as said below
- train_slot: int32 [64], replicated, may hold values from 0 to 63, as said below
- stem_weight: bfloat16 [81, 128], replicated, may hold values from -0.625 to 0.625
- stem_gain: float32 [128], replicated, may hold values from 0.1 to 1.9
- stem_shift: float32 [128], replicated, may hold values from -3 to 3
- mixer_weight: bfloat16 [3, 3, 384, 256], replicated, may hold values from -0.109375 to 0.109375
- mixer_gain: float32 [256], replicated, may hold values from 0.1 to 1.9
- mixer_shift: float32 [256], replicated, may hold values from -3 to 3
- down_weight: bfloat16 [1024, 256], replicated, may hold values from -0.1875 to 0.1875
- down_bias: float32 [256], replicated, may hold values from -3 to 3
Outputs:
- latents: bfloat16 [64, 8, 8, 32, 256], P('clip', 'tm', 'row')
The draws below stay inside these ranges and needn't reach their ends.
Inputs may be any that keep to these rules, and one draw needn't show every extreme that they name: `keep_list`: each encoder position 0 to 63 is named by exactly one slot, and -1 marks a dropped slot; encoder position e belongs to index e // 4 of clip. `train_slot`: A permutation; training position t belongs to index t // 4 of clip; at most 1 encoder positions of one index of clip go to one index of clip.
All inputs are finite; a program needn't handle non-finite values.
Results may differ from the reference program's by a relative error of at most 0.0053.
Values may be sent and summed in bfloat16 or wider, within the bound.
No kernel may reach another device: no remote copies, remote signals or barrier semaphores. Data moves between devices by JAX's collectives and lax.ppermute only.
A program may use at most 64 MiB of HBM per device.

```python
import jax
import jax.numpy as jnp
from jax import lax

C_IN = 3
C_MID = 128
C_OUT = 256
GROUPS = 32
SLOTS_DEV = 8
ENC_DEV = 4
COLS = 64
SLOTS = 128
TRAIN = 64
FRAMES = 16
ROWS = 16


def draw_frames(key, part):
    noise_key, offset_key = jax.random.split(key)
    time_pos = jnp.arange(FRAMES, dtype=jnp.float32) / max(FRAMES - 1, 1)
    row_pos = (jnp.arange(ROWS * COLS) // COLS).astype(jnp.float32) / max(ROWS - 1, 1)
    ramp = 0.5 + 0.5 * (time_pos[:, None] + row_pos[None, :])
    shape_full = (SLOTS, C_IN, FRAMES, ROWS * COLS)
    noise = jax.random.normal(noise_key, shape_full, jnp.float32)
    offset = 0.3 * jax.random.normal(offset_key, (SLOTS, C_IN), jnp.float32)
    return jnp.clip(offset[:, :, None, None] + ramp * noise, -6.0, 6.0).astype(jnp.bfloat16)


def draw_keep_list(key, part):
    busy_key, rank_key, place_key = jax.random.split(jax.random.fold_in(key, 11), 3)
    group_count = SLOTS // SLOTS_DEV
    busiest = jax.random.randint(busy_key, (), 0, group_count)
    ranks = jax.random.permutation(rank_key, SLOTS).astype(jnp.int32)
    slot_ids = jnp.arange(SLOTS, dtype=jnp.int32)
    score = jnp.where(slot_ids // SLOTS_DEV == busiest, slot_ids % SLOTS_DEV - SLOTS_DEV, ranks)
    order = jnp.argsort(score, stable=True)
    chosen = order[:TRAIN]
    positions = jax.random.permutation(place_key, TRAIN).astype(jnp.int32)
    return jnp.full((SLOTS,), -1, jnp.int32).at[chosen].set(positions)


def draw_train_slot(key, part):
    keys = jax.random.split(jax.random.fold_in(key, 23), 5)
    group_count = TRAIN // ENC_DEV
    outer = jax.random.permutation(keys[0], group_count).astype(jnp.int32)
    inner = jax.random.permutation(keys[1], group_count).astype(jnp.int32)
    offsets = jax.random.permutation(keys[2], group_count).astype(jnp.int32)
    turn = jax.random.randint(keys[3], (group_count,), 0, ENC_DEV).astype(jnp.int32)
    positions = jnp.arange(TRAIN, dtype=jnp.int32)
    sender = positions // ENC_DEV
    within = (positions % ENC_DEV + turn[sender]) % ENC_DEV
    destination = outer[(inner[sender] + offsets[within % group_count]) % group_count]
    score = jax.random.permutation(keys[4], TRAIN).astype(jnp.int32)
    same = destination[None, :] == destination[:, None]
    lower = score[None, :] < score[:, None]
    landing = jnp.sum((same & lower).astype(jnp.int32), axis=1)
    return (destination * ENC_DEV + landing).astype(jnp.int32)


def gaussian(rng, dims, deviation, bound, kind=jnp.bfloat16):
    drawn = jax.random.normal(rng, dims, jnp.float32) * deviation
    return jnp.minimum(jnp.maximum(drawn, -bound), bound).astype(kind)


def setup_inputs(seed: int = 0) -> dict:
    key_of = jax.random.split(jax.random.key(seed), 12)
    frames = draw_frames(jax.random.fold_in(key_of[11], 71), 0)
    keep_list = draw_keep_list(jax.random.fold_in(key_of[11], 71), 0)
    train_slot = draw_train_slot(jax.random.fold_in(key_of[11], 71), 0)
    stem_weight = gaussian(key_of[3], (27 * C_IN, C_MID), (27 * C_IN) ** -0.5, 0.625)
    stem_gain = jnp.clip(1.0 + 0.18 * jax.random.normal(key_of[4], (C_MID,), jnp.float32), 0.1, 1.9)
    stem_shift = gaussian(key_of[5], (C_MID,), 0.5, 3.0, jnp.float32)
    mixer_weight = gaussian(key_of[6], (3, 3, 3 * C_MID, C_OUT), (27 * C_MID) ** -0.5, 0.109375)
    mixer_gain = jnp.clip(1.0 + 0.18 * jax.random.normal(key_of[7], (C_OUT,), jnp.float32), 0.1, 1.9)
    mixer_shift = gaussian(key_of[8], (C_OUT,), 0.5, 3.0, jnp.float32)
    down_weight = gaussian(key_of[9], (4 * C_OUT, C_OUT), (4 * C_OUT) ** -0.5, 0.1875)
    down_bias = gaussian(key_of[10], (C_OUT,), 0.5, 3.0, jnp.float32)
    return {"frames": frames, "keep_list": keep_list, "train_slot": train_slot, "stem_weight": stem_weight, "stem_gain": stem_gain, "stem_shift": stem_shift, "mixer_weight": mixer_weight, "mixer_gain": mixer_gain, "mixer_shift": mixer_shift, "down_weight": down_weight, "down_bias": down_bias}


eps = 1e-06

def product(left, right):
    return jnp.dot(left.astype(jnp.float32), right.astype(jnp.float32), precision=lax.Precision.HIGHEST)

def norm_silu(hidden, gain, shift):
    cell_n, chan_n = hidden.shape
    per_group = chan_n // GROUPS
    value_sum = lax.optimization_barrier(jnp.sum(hidden, axis=0)).reshape(GROUPS, per_group).sum(-1)
    square_sum = lax.optimization_barrier(jnp.sum(hidden * hidden, axis=0)).reshape(GROUPS, per_group).sum(-1)
    cell_count = cell_n * per_group
    group_mean = value_sum / cell_count
    spread = square_sum / cell_count - group_mean * group_mean
    inverse = lax.rsqrt(spread + eps)
    mean_full = jnp.repeat(group_mean, per_group)[None, :]
    scale_full = jnp.repeat(inverse, per_group)[None, :] * gain
    return jax.nn.silu((hidden - mean_full) * scale_full + shift)

def surround(volume):
    extended = jnp.concatenate([volume[:1], volume[:1], volume], axis=0)
    return jnp.pad(extended, ((0, 0), (1, 1), (1, 1), (0, 0)))

def encode_clip(clip, stem_weight, stem_gain, stem_shift, mixer_weight, mixer_gain, mixer_shift, down_weight, down_bias):
    volume = clip.reshape(C_IN, FRAMES, ROWS, COLS).transpose(1, 2, 3, 0)
    padded = surround(volume)
    tap_views = []
    for time_tap in range(3):
        for row_tap in range(3):
            for col_tap in range(3):
                tap_views.append(padded[time_tap:time_tap + FRAMES, row_tap:row_tap + ROWS, col_tap:col_tap + COLS])
    patches = jnp.concatenate(tap_views, axis=-1).reshape(FRAMES * ROWS * COLS, 27 * C_IN)
    stem = product(patches, stem_weight)
    hidden = norm_silu(stem, stem_gain, stem_shift).astype(jnp.bfloat16)
    padded = surround(hidden.reshape(FRAMES, ROWS, COLS, -1))
    accumulated = jnp.zeros((FRAMES * ROWS * COLS, mixer_weight.shape[3]), jnp.float32)
    for time_tap in range(3):
        for row_tap in range(3):
            tap_strip = jnp.concatenate([padded[time_tap:time_tap + FRAMES, row_tap:row_tap + ROWS, col_tap:col_tap + COLS] for col_tap in range(3)], axis=-1)
            accumulated = accumulated + product(tap_strip.reshape(-1, tap_strip.shape[-1]), mixer_weight[time_tap, row_tap])
    activated = norm_silu(accumulated, mixer_gain, mixer_shift).astype(jnp.bfloat16)
    activated = activated.reshape(FRAMES, ROWS, COLS, -1)
    pooled = ((activated[0::2].astype(jnp.float32) + activated[1::2].astype(jnp.float32)) * 0.5).astype(jnp.bfloat16)
    chan_out = pooled.shape[-1]
    blocks = pooled.reshape(FRAMES // 2, ROWS // 2, 2, COLS // 2, 2, chan_out).transpose(0, 1, 3, 2, 4, 5).reshape(-1, 4 * chan_out)
    latent = product(blocks, down_weight) + down_bias
    return latent.astype(jnp.bfloat16).reshape(FRAMES // 2, ROWS // 2, COLS // 2, chan_out)

def reference(frames, keep_list, train_slot, stem_weight, stem_gain, stem_shift, mixer_weight, mixer_gain, mixer_shift, down_weight, down_bias):
    target = jnp.where(keep_list >= 0, keep_list, TRAIN).astype(jnp.int32)
    slot_of_encoder = jnp.zeros((TRAIN,), jnp.int32).at[target].set(jnp.arange(SLOTS, dtype=jnp.int32), mode='drop')
    encoder_of_train = jnp.zeros((TRAIN,), jnp.int32).at[train_slot].set(jnp.arange(TRAIN, dtype=jnp.int32))
    source = slot_of_encoder[encoder_of_train]

    def encode_one(slot_index):
        clip = lax.dynamic_index_in_dim(frames, slot_index, 0, keepdims=False)
        return encode_clip(clip, stem_weight, stem_gain, stem_shift, mixer_weight, mixer_gain, mixer_shift, down_weight, down_bias)
    return lax.map(encode_one, source)
```

```python
import jax
import jax.numpy as jnp
import numpy as np
from jax import lax
from jax.experimental import pallas as pl
from jax.experimental.pallas import tpu as pltpu
from jax.sharding import PartitionSpec as P

GROUPS = 32
COLS = 64
F32 = jnp.float32
BF16 = jnp.bfloat16
eps = 1e-06

VMEM = pl.BlockSpec(memory_space=pltpu.VMEM)
SMEM = pl.BlockSpec(memory_space=pltpu.SMEM)


def iota(shape, dim):
    return lax.broadcasted_iota(jnp.int32, shape, dim)


def pack_kernel(core_ref, keep_a, keep_b, train_ref, fr_a, fr_b, out_ref):
    out_ref[...] = jnp.zeros_like(out_ref)
    core = core_ref[0]
    for keep_ref, fr in ((keep_a, fr_a), (keep_b, fr_b)):
        for j in range(fr.shape[0]):
            k = keep_ref[j]
            t = train_ref[jnp.maximum(k, 0)]
            mine = jnp.logical_and(k >= 0, ((t >> 2) & 1) == core)

            @pl.when(mine)
            def _():
                out_ref[t >> 3, t & 3] = fr[j]


def combine_kernel(recv_ref, out_ref, rows_ref):
    for k in range(4):
        for ch in range(3):
            total = recv_ref[0, k, ch].astype(F32)
            for s in range(1, recv_ref.shape[0]):
                total = total + recv_ref[s, k, ch].astype(F32)
            at = (k * 3 + ch) * 4
            rows_ref[at : at + 4, :] = total
    i = iota((256, 256), 0)
    o = iota((256, 256), 1)
    source = ((o >> 5) & 3) * 64 + (o & 31) * 2 + (o >> 7)
    pick = (i == source).astype(F32).astype(BF16)
    split = jnp.dot(rows_ref[...].astype(BF16), pick, preferred_element_type=F32)
    rows_ref[...] = split
    for k in range(4):
        for ch in range(3):
            at = (k * 3 + ch) * 4
            piece = rows_ref[at : at + 4, :].astype(BF16)
            for y in range(4):
                out_ref[y * 4 + k, ch] = piece


def group_scale(total, square, cells, per_group, gain, shift):
    n = total.shape[1]
    gi = iota((n, n), 0) // per_group
    gj = iota((n, n), 1) // per_group
    member = (gi == gj).astype(F32)
    both = jnp.concatenate([total, square, jnp.zeros((6, n), F32)], axis=0)
    sums = jnp.dot(both, member, precision=lax.Precision.HIGHEST, preferred_element_type=F32)
    sums = sums * (1.0 / (cells * per_group))
    mean = sums[0:1]
    spread = sums[1:2] - mean * mean
    scale = gain * lax.rsqrt(spread + eps)
    return scale, shift - mean * scale


def silu(u):
    half = 0.5 * u
    return half + half * jnp.tanh(half)


def mixer_kernel(
    y_ref, raw_ref, w4_ref, gain_ref, shift_ref, mw_ref, mix_ref, stat_ref, dv, tg, stem, hid
):
    y = y_ref[0]
    for yy in range(4):
        for xx in range(4):
            for ch in range(3):
                piece = raw_ref[yy * 4 + xx, ch].astype(F32)
                for par in range(2):
                    dv[1 + par, ch, 4 + 4 * xx : 8 + 4 * xx, 128 * yy : 128 * yy + 128] = piece[
                        :, 128 * par : 128 * par + 128
                    ]
    pair = iota((16, 512), 1) & 31
    for ch in range(3):
        even = dv[1, ch, 4:20, :]
        odd = dv[2, ch, 4:20, :]
        dv[0, ch, 4:20, :] = jnp.where(pair == 0, 0.0, pltpu.roll(odd, 1, 1))
        dv[3, ch, 4:20, :] = jnp.where(pair == 31, 0.0, pltpu.roll(even, 511, 1))
    for v in range(4):
        for ch in range(3):
            dv[v, ch, 0:4, :] = jnp.broadcast_to(dv[v, ch, 4:5, :], (4, 512))
    edge = jnp.zeros((32, 128), BF16)
    for g in range(4):
        tg[g, 0:32, :] = edge
        tg[g, 544:576, :] = edge
        rows = [dv[v, ch, 4 * g : 4 * g + 8, :] for v in range(4) for ch in range(3)]
        block = jnp.concatenate(rows + [jnp.zeros((32, 512), F32)], axis=0)
        tg[g, 32:544, :] = jnp.transpose(block).astype(BF16)
    total = jnp.zeros((8, 1024), F32)
    square = jnp.zeros((8, 1024), F32)
    for g in range(4):
        stem[g, 0:32, :] = jnp.zeros((32, 1024), F32)
        stem[g, 544:576, :] = jnp.zeros((32, 1024), F32)
        left = jnp.concatenate([tg[g, 32 * b : 32 * b + 512, :] for b in range(3)], axis=1)
        out = jnp.dot(left, w4_ref[...], preferred_element_type=F32)
        stem[g, 32:544, :] = out
        parts = out.reshape(64, 8, 1024)
        total = total + jnp.sum(parts, axis=0)
        square = square + jnp.sum(parts * parts, axis=0)
    total = jnp.sum(total, axis=0, keepdims=True)
    square = jnp.sum(square, axis=0, keepdims=True)
    total = sum(total[:, 128 * k : 128 * k + 128] for k in range(8))
    square = sum(square[:, 128 * k : 128 * k + 128] for k in range(8))
    scale, offset = group_scale(total, square, 16384, 4, gain_ref[...], shift_ref[...])
    at = iota((192, 128), 0)
    row = at >> 5
    valid = jnp.logical_and(
        jnp.logical_or(row > 0, y > 0), jnp.logical_or(row < 5, y < 3)
    )
    first = (at & 31) == 0
    last = (at & 31) == 31
    start = pl.multiple_of(y * 128, 128)
    for f in range(16):
        g, fo = divmod(f, 4)
        val = stem[g, pl.ds(start, 192), 256 * fo : 256 * fo + 256]
        even = jnp.where(valid, silu(val[:, :128] * scale + offset), 0.0)
        odd = jnp.where(valid, silu(val[:, 128:] * scale + offset), 0.0)
        before = jnp.where(first, 0.0, pltpu.roll(odd, 1, 0))
        after = jnp.where(last, 0.0, pltpu.roll(even, 191, 0))
        for k, part in enumerate((before, even, odd, after)):
            part = part.astype(BF16)
            hid[f + 2, :, 128 * k : 128 * k + 128] = part
            if f == 0:
                hid[0, :, 128 * k : 128 * k + 128] = part
                hid[1, :, 128 * k : 128 * k + 128] = part

    def frame(f, carry):
        s, q = carry
        for par in range(2):
            taps = [
                hid[f + a, 32 * b : 32 * b + 128, 128 * par : 128 * par + 384]
                for a in range(3)
                for b in range(3)
            ]
            left = jnp.concatenate(taps, axis=1)
            out = jnp.dot(left, mw_ref[...], preferred_element_type=F32)
            mix_ref[par, f] = out
            parts = out.reshape(16, 8, 256)
            s = s + jnp.sum(parts, axis=0)
            q = q + jnp.sum(parts * parts, axis=0)
        return s, q

    zero = jnp.zeros((8, 256), F32)
    s, q = lax.fori_loop(0, 16, frame, (zero, zero))
    stat_ref[0:1, :] = jnp.sum(s, axis=0, keepdims=True)
    stat_ref[1:2, :] = jnp.sum(q, axis=0, keepdims=True)


def down_kernel(mix_ref, stat_ref, gain_ref, shift_ref, dw_ref, bias_ref, out_ref, left):
    scale, offset = group_scale(
        stat_ref[0:1, :], stat_ref[1:2, :], 16384, 8, gain_ref[...], shift_ref[...]
    )
    for g in range(8):
        for par in range(2):
            one = silu(mix_ref[par, 2 * g] * scale + offset)
            two = silu(mix_ref[par, 2 * g + 1] * scale + offset)
            pooled = ((one + two) * 0.5).astype(BF16)
            for r in range(4):
                lane = ((r & 1) * 2 + par) * 256
                to = g * 64 + (r >> 1) * 32
                left[to : to + 32, lane : lane + 256] = pooled[32 * r : 32 * r + 32]
    out = jnp.dot(left[...], dw_ref[...], preferred_element_type=F32) + bias_ref[...]
    out_ref[...] = out.astype(BF16)


def stem_places():
    place = np.zeros((8, 3, 128, 81), np.float32)
    for fo in range(4):
        for par in range(2):
            for a in range(3):
                for b in range(3):
                    for c in range(3):
                        for ch in range(3):
                            row = (par + c) * 24 + ch * 8 + fo + 2 + a
                            place[fo * 2 + par, b, row, ((a * 3 + b) * 3 + c) * 3 + ch] = 1
    return place.reshape(8, 384, 81)


def call(kernel, out_shape, specs, scratch=(), mib=48):
    return pl.pallas_call(
        kernel,
        out_shape=out_shape,
        in_specs=specs,
        out_specs=jax.tree.map(lambda _: VMEM, out_shape),
        scratch_shapes=list(scratch),
        compiler_params=pltpu.CompilerParams(vmem_limit_bytes=mib << 20),
    )


def local(
    frames,
    keep_list,
    train_slot,
    stem_weight,
    stem_gain,
    stem_shift,
    mixer_weight,
    mixer_gain,
    mixer_shift,
    down_weight,
    down_bias,
):
    sds = jax.ShapeDtypeStruct
    index = lax.axis_index("clip")
    core = (index % 2).astype(jnp.int32).reshape(1)
    row = lax.axis_index("row").astype(jnp.int32).reshape(1)
    pairs = [(i, i ^ 1) for i in range(16)]
    frames_b = lax.ppermute(frames, "clip", pairs)
    keep_b = lax.ppermute(keep_list, "clip", pairs)
    packed = call(
        pack_kernel, sds((8, 4, 3, 4, 256), BF16), [SMEM] * 4 + [VMEM] * 2
    )(core, keep_list, keep_b, train_slot, frames, frames_b)
    along_z = [[2 * z + k for z in range(8)] for k in range(2)]
    received = lax.all_to_all(
        packed, "clip", split_axis=0, concat_axis=0, tiled=True, axis_index_groups=along_z
    )
    pieces = call(
        combine_kernel, sds((16, 3, 4, 256), BF16), [VMEM], [pltpu.VMEM((48, 256), F32)]
    )(received)
    raw = lax.all_to_all(pieces, ("row", "tm"), split_axis=0, concat_axis=0, tiled=True)
    places = jnp.asarray(stem_places(), BF16)
    w4 = jnp.einsum("nkp,pc->knc", places, stem_weight).reshape(384, 1024)
    mix, stat = call(
        mixer_kernel,
        (sds((2, 16, 128, 256), F32), sds((2, 256), F32)),
        [SMEM] + [VMEM] * 5,
        [
            pltpu.VMEM((4, 3, 24, 512), F32),
            pltpu.VMEM((4, 576, 128), BF16),
            pltpu.VMEM((4, 576, 1024), F32),
            pltpu.VMEM((18, 192, 512), BF16),
        ],
    )(
        row,
        raw,
        w4,
        stem_gain.reshape(1, -1),
        stem_shift.reshape(1, -1),
        mixer_weight.reshape(3456, 256),
    )
    stat = lax.psum(stat, "row")
    latent = call(
        down_kernel, sds((512, 256), BF16), [VMEM] * 6, [pltpu.VMEM((512, 1024), BF16)]
    )(
        mix,
        stat,
        mixer_gain.reshape(1, -1),
        mixer_shift.reshape(1, -1),
        down_weight,
        down_bias.reshape(1, -1),
    )
    return lax.all_to_all(
        latent.reshape(4, 2, 2, 32, 256), "tm", split_axis=0, concat_axis=0, tiled=True
    )


def solution(mesh):
    return jax.shard_map(
        local,
        mesh=mesh,
        in_specs=(P("clip", None, "tm", "row"), P("clip")) + (P(),) * 9,
        out_specs=P("clip", "tm", "row", None, None),
        check_vma=False,
    )
```

```python
import jax
import jax.numpy as jnp
import numpy as np
from jax import lax
from jax.experimental import pallas as pl
from jax.experimental.pallas import tpu as pltpu
from jax.sharding import PartitionSpec as P

GROUPS = 32
COLS = 64
F32 = jnp.float32
BF16 = jnp.bfloat16
eps = 1e-06

VMEM = pl.BlockSpec(memory_space=pltpu.VMEM)
SMEM = pl.BlockSpec(memory_space=pltpu.SMEM)
ANY = pl.BlockSpec(memory_space=pl.ANY)
HBM = pl.BlockSpec(memory_space=pltpu.HBM)


def iota(shape, dim):
    return lax.broadcasted_iota(jnp.int32, shape, dim)


def pack_kernel(
    core_ref, keep_a, keep_b, train, fr_a, fr_b, out_ref, keep_s, keep_t, train_s, fra, frb, sems
):
    pairs = ((keep_a, keep_s), (keep_b, keep_t), (train, train_s), (fr_a, fra), (fr_b, frb))
    copies = [pltpu.make_async_copy(src, dst, sems.at[i]) for i, (src, dst) in enumerate(pairs)]
    for copy in copies:
        copy.start()
    out_ref[...] = jnp.zeros_like(out_ref)
    for copy in copies:
        copy.wait()
    core = core_ref[0]
    for keep_ref, fr in ((keep_s, fra), (keep_t, frb)):
        for j in range(fr.shape[0]):
            k = keep_ref[j]
            t = train_s[jnp.maximum(k, 0)]
            mine = jnp.logical_and(k >= 0, ((t >> 2) & 1) == core)

            @pl.when(mine)
            def _():
                out_ref[t >> 3, t & 3] = fr[j]


def combine_kernel(recv_ref, out_ref, rows_ref):
    for k in range(4):
        for ch in range(3):
            total = recv_ref[0, k, ch].astype(F32)
            for s in range(1, recv_ref.shape[0]):
                total = total + recv_ref[s, k, ch].astype(F32)
            at = (k * 3 + ch) * 4
            rows_ref[at : at + 4, :] = total
    i = iota((256, 256), 0)
    o = iota((256, 256), 1)
    source = ((o >> 5) & 3) * 64 + (o & 31) * 2 + (o >> 7)
    pick = (i == source).astype(F32).astype(BF16)
    split = jnp.dot(rows_ref[...].astype(BF16), pick, preferred_element_type=F32)
    rows_ref[...] = split
    for k in range(4):
        for ch in range(3):
            at = (k * 3 + ch) * 4
            piece = rows_ref[at : at + 4, :].astype(BF16)
            for y in range(4):
                out_ref[y * 4 + k, ch] = piece


def group_scale(total, square, cells, per_group, gain, shift):
    n = total.shape[1]
    gi = iota((n, n), 0) // per_group
    gj = iota((n, n), 1) // per_group
    member = (gi == gj).astype(F32)
    both = jnp.concatenate([total, square, jnp.zeros((6, n), F32)], axis=0)
    sums = jnp.dot(both, member, precision=lax.Precision.HIGHEST, preferred_element_type=F32)
    sums = sums * (1.0 / (cells * per_group))
    mean = sums[0:1]
    spread = sums[1:2] - mean * mean
    scale = gain * lax.rsqrt(spread + eps)
    return scale, shift - mean * scale


def silu(u):
    half = 0.5 * u
    return half + half * jnp.tanh(half)


def mixer_kernel(
    y_ref,
    raw_ref,
    w4_ref,
    gain_hbm,
    shift_hbm,
    mw_ref,
    mix_ref,
    stat_ref,
    dv,
    tg,
    stem,
    hid,
    gain_ref,
    shift_ref,
    sems,
):
    y = y_ref[0]
    copies = [
        pltpu.make_async_copy(gain_hbm, gain_ref, sems.at[0]),
        pltpu.make_async_copy(shift_hbm, shift_ref, sems.at[1]),
    ]
    for copy in copies:
        copy.start()
    for yy in range(4):
        for xx in range(4):
            for ch in range(3):
                piece = raw_ref[yy * 4 + xx, ch].astype(F32)
                for par in range(2):
                    dv[1 + par, ch, 4 + 4 * xx : 8 + 4 * xx, 128 * yy : 128 * yy + 128] = piece[
                        :, 128 * par : 128 * par + 128
                    ]
    pair = iota((16, 512), 1) & 31
    for ch in range(3):
        even = dv[1, ch, 4:20, :]
        odd = dv[2, ch, 4:20, :]
        dv[0, ch, 4:20, :] = jnp.where(pair == 0, 0.0, pltpu.roll(odd, 1, 1))
        dv[3, ch, 4:20, :] = jnp.where(pair == 31, 0.0, pltpu.roll(even, 511, 1))
    for v in range(4):
        for ch in range(3):
            dv[v, ch, 0:4, :] = jnp.broadcast_to(dv[v, ch, 4:5, :], (4, 512))
    edge = jnp.zeros((32, 128), BF16)
    for g in range(4):
        tg[g, 0:32, :] = edge
        tg[g, 544:576, :] = edge
        rows = [dv[v, ch, 4 * g : 4 * g + 8, :] for v in range(4) for ch in range(3)]
        block = jnp.concatenate(rows + [jnp.zeros((32, 512), F32)], axis=0)
        tg[g, 32:544, :] = jnp.transpose(block).astype(BF16)
    total = jnp.zeros((8, 1024), F32)
    square = jnp.zeros((8, 1024), F32)
    for g in range(4):
        stem[g, 0:32, :] = jnp.zeros((32, 1024), F32)
        stem[g, 544:576, :] = jnp.zeros((32, 1024), F32)
        left = jnp.concatenate([tg[g, 32 * b : 32 * b + 512, :] for b in range(3)], axis=1)
        w4 = jnp.concatenate([w4_ref[n] for n in range(8)], axis=1)
        out = jnp.dot(left, w4, preferred_element_type=F32)
        stem[g, 32:544, :] = out
        parts = out.reshape(64, 8, 1024)
        total = total + jnp.sum(parts, axis=0)
        square = square + jnp.sum(parts * parts, axis=0)
    total = jnp.sum(total, axis=0, keepdims=True)
    square = jnp.sum(square, axis=0, keepdims=True)
    total = sum(total[:, 128 * k : 128 * k + 128] for k in range(8))
    square = sum(square[:, 128 * k : 128 * k + 128] for k in range(8))
    for copy in copies:
        copy.wait()
    scale, offset = group_scale(total, square, 16384, 4, gain_ref[...], shift_ref[...])
    at = iota((192, 128), 0)
    row = at >> 5
    valid = jnp.logical_and(
        jnp.logical_or(row > 0, y > 0), jnp.logical_or(row < 5, y < 3)
    )
    first = (at & 31) == 0
    last = (at & 31) == 31
    start = pl.multiple_of(y * 128, 128)
    for f in range(16):
        g, fo = divmod(f, 4)
        val = stem[g, pl.ds(start, 192), 256 * fo : 256 * fo + 256]
        even = jnp.where(valid, silu(val[:, :128] * scale + offset), 0.0)
        odd = jnp.where(valid, silu(val[:, 128:] * scale + offset), 0.0)
        before = jnp.where(first, 0.0, pltpu.roll(odd, 1, 0))
        after = jnp.where(last, 0.0, pltpu.roll(even, 191, 0))
        for k, part in enumerate((before, even, odd, after)):
            part = part.astype(BF16)
            hid[f + 2, :, 128 * k : 128 * k + 128] = part
            if f == 0:
                hid[0, :, 128 * k : 128 * k + 128] = part
                hid[1, :, 128 * k : 128 * k + 128] = part

    def frame(f, carry):
        s, q = carry
        for par in range(2):
            taps = [
                hid[f + a, 32 * b : 32 * b + 128, 128 * par : 128 * par + 384]
                for a in range(3)
                for b in range(3)
            ]
            left = jnp.concatenate(taps, axis=1)
            out = jnp.dot(left, mw_ref[...], preferred_element_type=F32)
            mix_ref[par, f] = out
            parts = out.reshape(16, 8, 256)
            s = s + jnp.sum(parts, axis=0)
            q = q + jnp.sum(parts * parts, axis=0)
        return s, q

    zero = jnp.zeros((8, 256), F32)
    s, q = lax.fori_loop(0, 16, frame, (zero, zero))
    stat_ref[0:1, :] = jnp.sum(s, axis=0, keepdims=True)
    stat_ref[1:2, :] = jnp.sum(q, axis=0, keepdims=True)


def down_kernel(mix_ref, stat_a, stat_b, stat_c, stat_d, gain_ref, shift_ref, dw_ref, bias_ref, out_ref, left):
    stat = (stat_a[...] + stat_b[...]) + (stat_c[...] + stat_d[...])
    scale, offset = group_scale(
        stat[0:1, :], stat[1:2, :], 16384, 8, gain_ref[...], shift_ref[...]
    )
    for g in range(8):
        for par in range(2):
            one = silu(mix_ref[par, 2 * g] * scale + offset)
            two = silu(mix_ref[par, 2 * g + 1] * scale + offset)
            pooled = ((one + two) * 0.5).astype(BF16)
            for r in range(4):
                lane = ((r & 1) * 2 + par) * 256
                to = g * 64 + (r >> 1) * 32
                left[to : to + 32, lane : lane + 256] = pooled[32 * r : 32 * r + 32]
    out = jnp.dot(left[...], dw_ref[...], preferred_element_type=F32) + bias_ref[...]
    out_ref[...] = out.astype(BF16)


def stem_places():
    place = np.zeros((8, 3, 128, 81), np.float32)
    for fo in range(4):
        for par in range(2):
            for a in range(3):
                for b in range(3):
                    for c in range(3):
                        for ch in range(3):
                            row = (par + c) * 24 + ch * 8 + fo + 2 + a
                            place[fo * 2 + par, b, row, ((a * 3 + b) * 3 + c) * 3 + ch] = 1
    return place.reshape(3072, 81)


def call(kernel, out_shape, specs, scratch=(), mib=16):
    return pl.pallas_call(
        kernel,
        out_shape=out_shape,
        in_specs=specs,
        out_specs=jax.tree.map(lambda _: VMEM, out_shape),
        scratch_shapes=list(scratch),
        compiler_params=pltpu.CompilerParams(vmem_limit_bytes=mib << 20),
    )


def local(
    frames,
    keep_list,
    train_slot,
    stem_weight,
    stem_gain,
    stem_shift,
    mixer_weight,
    mixer_gain,
    mixer_shift,
    down_weight,
    down_bias,
):
    sds = jax.ShapeDtypeStruct
    index = lax.axis_index("clip")
    core = (index % 2).astype(jnp.int32).reshape(1)
    row = lax.axis_index("row").astype(jnp.int32).reshape(1)
    pairs = [(i, i ^ 1) for i in range(16)]
    frames_b = lax.ppermute(frames, "clip", pairs)
    keep_b = lax.ppermute(keep_list, "clip", pairs)
    packed = call(
        pack_kernel,
        sds((8, 4, 3, 4, 256), BF16),
        [SMEM, HBM, ANY, HBM, HBM, ANY],
        [
            pltpu.SMEM((8,), jnp.int32),
            pltpu.SMEM((8,), jnp.int32),
            pltpu.SMEM((64,), jnp.int32),
            pltpu.VMEM((8, 3, 4, 256), BF16),
            pltpu.VMEM((8, 3, 4, 256), BF16),
            pltpu.SemaphoreType.DMA((5,)),
        ],
    )(core, keep_list, keep_b, train_slot, frames, frames_b)
    along_z = [[2 * z + k for z in range(8)] for k in range(2)]
    received = lax.all_to_all(
        packed, "clip", split_axis=0, concat_axis=0, tiled=True, axis_index_groups=along_z
    )
    pieces = call(
        combine_kernel, sds((16, 3, 4, 256), BF16), [VMEM], [pltpu.VMEM((48, 256), F32)]
    )(received)
    places = jnp.asarray(stem_places(), BF16)
    w4 = jnp.dot(places, stem_weight, preferred_element_type=F32).astype(BF16)
    pieces, w4 = lax.optimization_barrier((pieces, w4))
    raw = lax.all_to_all(pieces, ("row", "tm"), split_axis=0, concat_axis=0, tiled=True)
    mix, stat = call(
        mixer_kernel,
        (sds((2, 16, 128, 256), F32), sds((2, 256), F32)),
        [SMEM, VMEM, VMEM, HBM, HBM, VMEM],
        [
            pltpu.VMEM((4, 3, 24, 512), F32),
            pltpu.VMEM((4, 576, 128), BF16),
            pltpu.VMEM((4, 576, 1024), F32),
            pltpu.VMEM((18, 192, 512), BF16),
            pltpu.VMEM((1, 128), F32),
            pltpu.VMEM((1, 128), F32),
            pltpu.SemaphoreType.DMA((2,)),
        ],
        mib=24,
    )(
        row,
        raw,
        w4.reshape(8, 384, 128),
        stem_gain.reshape(1, -1),
        stem_shift.reshape(1, -1),
        mixer_weight.reshape(3456, 256),
    )
    others = [
        lax.ppermute(stat, "row", [(i, (i + by) % 4) for i in range(4)]) for by in (1, 2, 3)
    ]
    latent = call(
        down_kernel, sds((512, 256), BF16), [VMEM] * 9, [pltpu.VMEM((512, 1024), BF16)], mib=16
    )(
        mix,
        stat,
        *others,
        mixer_gain.reshape(1, -1),
        mixer_shift.reshape(1, -1),
        down_weight,
        down_bias.reshape(1, -1),
    )
    return lax.all_to_all(
        latent.reshape(4, 2, 2, 32, 256), "tm", split_axis=0, concat_axis=0, tiled=True
    )


def solution(mesh):
    return jax.shard_map(
        local,
        mesh=mesh,
        in_specs=(P("clip", None, "tm", "row"), P("clip")) + (P(),) * 9,
        out_specs=P("clip", "tm", "row", None, None),
        check_vma=False,
    )
```

```python
import jax
import jax.numpy as jnp
import numpy as np
from jax import lax
from jax.experimental import pallas as pl
from jax.experimental.pallas import tpu as pltpu
from jax.sharding import PartitionSpec as P

GROUPS = 32
COLS = 64
F32 = jnp.float32
BF16 = jnp.bfloat16
eps = 1e-06

VMEM = pl.BlockSpec(memory_space=pltpu.VMEM)
SMEM = pl.BlockSpec(memory_space=pltpu.SMEM)
ANY = pl.BlockSpec(memory_space=pl.ANY)
HBM = pl.BlockSpec(memory_space=pltpu.HBM)


def iota(shape, dim):
    return lax.broadcasted_iota(jnp.int32, shape, dim)


def pack_kernel(
    core_ref, keep_a, keep_b, train, fr_a, fr_b, out_ref, keep_s, keep_t, train_s, fra, frb, sems
):
    pairs = ((keep_a, keep_s), (keep_b, keep_t), (train, train_s), (fr_a, fra), (fr_b, frb))
    copies = [pltpu.make_async_copy(src, dst, sems.at[i]) for i, (src, dst) in enumerate(pairs)]
    for copy in copies:
        copy.start()
    out_ref[...] = jnp.zeros_like(out_ref)
    for copy in copies:
        copy.wait()
    core = core_ref[0]
    for keep_ref, fr in ((keep_s, fra), (keep_t, frb)):
        for j in range(fr.shape[0]):
            k = keep_ref[j]
            t = train_s[jnp.maximum(k, 0)]
            mine = jnp.logical_and(k >= 0, ((t >> 2) & 1) == core)

            @pl.when(mine)
            def _():
                out_ref[t >> 3, t & 3] = fr[j]


def combine_kernel(recv_ref, out_ref, rows_ref):
    for k in range(4):
        for ch in range(3):
            total = recv_ref[0, k, ch].astype(F32)
            for s in range(1, recv_ref.shape[0]):
                total = total + recv_ref[s, k, ch].astype(F32)
            at = (k * 3 + ch) * 4
            rows_ref[at : at + 4, :] = total
    i = iota((256, 256), 0)
    o = iota((256, 256), 1)
    source = ((o >> 5) & 3) * 64 + (o & 31) * 2 + (o >> 7)
    pick = (i == source).astype(F32).astype(BF16)
    split = jnp.dot(rows_ref[...].astype(BF16), pick, preferred_element_type=F32)
    rows_ref[...] = split
    for k in range(4):
        for ch in range(3):
            at = (k * 3 + ch) * 4
            piece = rows_ref[at : at + 4, :].astype(BF16)
            for y in range(4):
                out_ref[y * 4 + k, ch] = piece


def group_scale(total, square, cells, per_group, gain, shift):
    n = total.shape[1]
    gi = iota((n, n), 0) // per_group
    gj = iota((n, n), 1) // per_group
    member = (gi == gj).astype(F32)
    both = jnp.concatenate([total, square, jnp.zeros((6, n), F32)], axis=0)
    sums = jnp.dot(both, member, precision=lax.Precision.HIGHEST, preferred_element_type=F32)
    sums = sums * (1.0 / (cells * per_group))
    mean = sums[0:1]
    spread = sums[1:2] - mean * mean
    scale = gain * lax.rsqrt(spread + eps)
    return scale, shift - mean * scale


def silu(u):
    half = 0.5 * u
    return half + half * jnp.tanh(half)


def mixer_kernel(
    y_ref,
    raw_ref,
    w4_ref,
    gain_hbm,
    shift_hbm,
    mw_ref,
    mix_ref,
    stat_ref,
    dv,
    tg,
    stem,
    hid,
    gain_ref,
    shift_ref,
    sems,
):
    y = y_ref[0]
    copies = [
        pltpu.make_async_copy(gain_hbm, gain_ref, sems.at[0]),
        pltpu.make_async_copy(shift_hbm, shift_ref, sems.at[1]),
    ]
    for copy in copies:
        copy.start()
    for yy in range(4):
        for xx in range(4):
            for ch in range(3):
                piece = raw_ref[yy * 4 + xx, ch].astype(F32)
                for par in range(2):
                    dv[1 + par, ch, 4 + 4 * xx : 8 + 4 * xx, 128 * yy : 128 * yy + 128] = piece[
                        :, 128 * par : 128 * par + 128
                    ]
    pair = iota((16, 512), 1) & 31
    for ch in range(3):
        even = dv[1, ch, 4:20, :]
        odd = dv[2, ch, 4:20, :]
        dv[0, ch, 4:20, :] = jnp.where(pair == 0, 0.0, pltpu.roll(odd, 1, 1))
        dv[3, ch, 4:20, :] = jnp.where(pair == 31, 0.0, pltpu.roll(even, 511, 1))
    for v in range(4):
        for ch in range(3):
            dv[v, ch, 0:4, :] = jnp.broadcast_to(dv[v, ch, 4:5, :], (4, 512))
    edge = jnp.zeros((32, 128), BF16)
    for g in range(4):
        tg[g, 0:32, :] = edge
        tg[g, 544:576, :] = edge
        rows = [dv[v, ch, 4 * g : 4 * g + 8, :] for v in range(4) for ch in range(3)]
        block = jnp.concatenate(rows + [jnp.zeros((32, 512), F32)], axis=0)
        tg[g, 32:544, :] = jnp.transpose(block).astype(BF16)
    total = jnp.zeros((8, 1024), F32)
    square = jnp.zeros((8, 1024), F32)
    for g in range(4):
        stem[g, 0:32, :] = jnp.zeros((32, 1024), F32)
        stem[g, 544:576, :] = jnp.zeros((32, 1024), F32)
        left = jnp.concatenate([tg[g, 32 * b : 32 * b + 512, :] for b in range(3)], axis=1)
        w4 = jnp.concatenate([w4_ref[n] for n in range(8)], axis=1)
        out = jnp.dot(left, w4, preferred_element_type=F32)
        stem[g, 32:544, :] = out
        parts = out.reshape(64, 8, 1024)
        total = total + jnp.sum(parts, axis=0)
        square = square + jnp.sum(parts * parts, axis=0)
    total = jnp.sum(total, axis=0, keepdims=True)
    square = jnp.sum(square, axis=0, keepdims=True)
    total = sum(total[:, 128 * k : 128 * k + 128] for k in range(8))
    square = sum(square[:, 128 * k : 128 * k + 128] for k in range(8))
    for copy in copies:
        copy.wait()
    scale, offset = group_scale(total, square, 16384, 4, gain_ref[...], shift_ref[...])
    at = iota((192, 128), 0)
    row = at >> 5
    valid = jnp.logical_and(
        jnp.logical_or(row > 0, y > 0), jnp.logical_or(row < 5, y < 3)
    )
    first = (at & 31) == 0
    last = (at & 31) == 31
    start = pl.multiple_of(y * 128, 128)
    for f in range(16):
        g, fo = divmod(f, 4)
        val = stem[g, pl.ds(start, 192), 256 * fo : 256 * fo + 256]
        even = jnp.where(valid, silu(val[:, :128] * scale + offset), 0.0)
        odd = jnp.where(valid, silu(val[:, 128:] * scale + offset), 0.0)
        before = jnp.where(first, 0.0, pltpu.roll(odd, 1, 0))
        after = jnp.where(last, 0.0, pltpu.roll(even, 191, 0))
        for k, part in enumerate((before, even, odd, after)):
            part = part.astype(BF16)
            hid[f + 2, :, 128 * k : 128 * k + 128] = part
            if f == 0:
                hid[0, :, 128 * k : 128 * k + 128] = part
                hid[1, :, 128 * k : 128 * k + 128] = part

    s = jnp.zeros((8, 256), F32)
    q = jnp.zeros((8, 256), F32)
    for f in range(0, 16, 4):
        for par in range(2):
            taps = [
                hid[f + a : f + a + 4, 32 * b : 32 * b + 128, 128 * par : 128 * par + 384]
                for a in range(3)
                for b in range(3)
            ]
            left = jnp.concatenate([tap.reshape(512, 384) for tap in taps], axis=1)
            out = jnp.dot(left, mw_ref[...], preferred_element_type=F32)
            mix_ref[par, f : f + 4] = out.reshape(4, 128, 256)
            parts = out.reshape(64, 8, 256)
            s = s + jnp.sum(parts, axis=0)
            q = q + jnp.sum(parts * parts, axis=0)
    stat_ref[0:1, :] = jnp.sum(s, axis=0, keepdims=True)
    stat_ref[1:2, :] = jnp.sum(q, axis=0, keepdims=True)


def down_kernel(mix_ref, stat_a, stat_b, stat_c, stat_d, gain_ref, shift_ref, dw_ref, bias_ref, out_ref, left):
    stat = (stat_a[...] + stat_b[...]) + (stat_c[...] + stat_d[...])
    scale, offset = group_scale(
        stat[0:1, :], stat[1:2, :], 16384, 8, gain_ref[...], shift_ref[...]
    )
    for g in range(8):
        for par in range(2):
            one = silu(mix_ref[par, 2 * g] * scale + offset)
            two = silu(mix_ref[par, 2 * g + 1] * scale + offset)
            pooled = ((one + two) * 0.5).astype(BF16)
            for r in range(4):
                lane = ((r & 1) * 2 + par) * 256
                to = g * 64 + (r >> 1) * 32
                left[to : to + 32, lane : lane + 256] = pooled[32 * r : 32 * r + 32]
    out = jnp.dot(left[...], dw_ref[...], preferred_element_type=F32) + bias_ref[...]
    out_ref[...] = out.astype(BF16)


def stem_places():
    place = np.zeros((8, 3, 128, 81), np.float32)
    for fo in range(4):
        for par in range(2):
            for a in range(3):
                for b in range(3):
                    for c in range(3):
                        for ch in range(3):
                            row = (par + c) * 24 + ch * 8 + fo + 2 + a
                            place[fo * 2 + par, b, row, ((a * 3 + b) * 3 + c) * 3 + ch] = 1
    return place.reshape(3072, 81)


def in_hbm(array):
    return pltpu.with_memory_space_constraint(array, pltpu.HBM)


def call(kernel, out_shape, specs, scratch=(), mib=16):
    return pl.pallas_call(
        kernel,
        out_shape=out_shape,
        in_specs=specs,
        out_specs=jax.tree.map(lambda _: VMEM, out_shape),
        scratch_shapes=list(scratch),
        compiler_params=pltpu.CompilerParams(vmem_limit_bytes=mib << 20),
    )


def local(
    frames,
    keep_list,
    train_slot,
    stem_weight,
    stem_gain,
    stem_shift,
    mixer_weight,
    mixer_gain,
    mixer_shift,
    down_weight,
    down_bias,
):
    sds = jax.ShapeDtypeStruct
    index = lax.axis_index("clip")
    core = (index % 2).astype(jnp.int32).reshape(1)
    row = lax.axis_index("row").astype(jnp.int32).reshape(1)
    pairs = [(i, i ^ 1) for i in range(16)]
    frames_b = lax.ppermute(frames, "clip", pairs)
    keep_b = lax.ppermute(keep_list, "clip", pairs)
    packed = call(
        pack_kernel,
        sds((8, 4, 3, 4, 256), BF16),
        [SMEM, HBM, ANY, HBM, HBM, ANY],
        [
            pltpu.SMEM((8,), jnp.int32),
            pltpu.SMEM((8,), jnp.int32),
            pltpu.SMEM((64,), jnp.int32),
            pltpu.VMEM((8, 3, 4, 256), BF16),
            pltpu.VMEM((8, 3, 4, 256), BF16),
            pltpu.SemaphoreType.DMA((5,)),
        ],
    )(core, in_hbm(keep_list), keep_b, in_hbm(train_slot), in_hbm(frames), frames_b)
    along_z = [[2 * z + k for z in range(8)] for k in range(2)]
    received = lax.all_to_all(
        packed, "clip", split_axis=0, concat_axis=0, tiled=True, axis_index_groups=along_z
    )
    pieces = call(
        combine_kernel, sds((16, 3, 4, 256), BF16), [VMEM], [pltpu.VMEM((48, 256), F32)]
    )(received)
    places = jnp.asarray(stem_places(), BF16)
    w4 = jnp.dot(places, stem_weight, preferred_element_type=F32).astype(BF16)
    pieces, w4 = lax.optimization_barrier((pieces, w4))
    raw = lax.all_to_all(pieces, ("row", "tm"), split_axis=0, concat_axis=0, tiled=True)
    mix, stat = call(
        mixer_kernel,
        (sds((2, 16, 128, 256), F32), sds((2, 256), F32)),
        [SMEM, VMEM, VMEM, HBM, HBM, VMEM],
        [
            pltpu.VMEM((4, 3, 24, 512), F32),
            pltpu.VMEM((4, 576, 128), BF16),
            pltpu.VMEM((4, 576, 1024), F32),
            pltpu.VMEM((18, 192, 512), BF16),
            pltpu.VMEM((1, 128), F32),
            pltpu.VMEM((1, 128), F32),
            pltpu.SemaphoreType.DMA((2,)),
        ],
        mib=24,
    )(
        row,
        raw,
        w4.reshape(8, 384, 128),
        in_hbm(stem_gain.reshape(1, -1)),
        in_hbm(stem_shift.reshape(1, -1)),
        mixer_weight.reshape(3456, 256),
    )
    others = [
        lax.ppermute(stat, "row", [(i, (i + by) % 4) for i in range(4)]) for by in (1, 2, 3)
    ]
    latent = call(
        down_kernel, sds((512, 256), BF16), [VMEM] * 9, [pltpu.VMEM((512, 1024), BF16)], mib=16
    )(
        mix,
        stat,
        *others,
        mixer_gain.reshape(1, -1),
        mixer_shift.reshape(1, -1),
        down_weight,
        down_bias.reshape(1, -1),
    )
    return lax.all_to_all(
        latent.reshape(4, 2, 2, 32, 256), "tm", split_axis=0, concat_axis=0, tiled=True
    )


def solution(mesh):
    return jax.shard_map(
        local,
        mesh=mesh,
        in_specs=(P("clip", None, "tm", "row"), P("clip")) + (P(),) * 9,
        out_specs=P("clip", "tm", "row", None, None),
        check_vma=False,
    )
```

```python
import jax
import jax.numpy as jnp
import numpy as np
from jax import lax
from jax.experimental import pallas as pl
from jax.experimental.pallas import tpu as pltpu
from jax.sharding import PartitionSpec as P

GROUPS = 32
COLS = 64
F32 = jnp.float32
BF16 = jnp.bfloat16
eps = 1e-06

VMEM = pl.BlockSpec(memory_space=pltpu.VMEM)
SMEM = pl.BlockSpec(memory_space=pltpu.SMEM)
ANY = pl.BlockSpec(memory_space=pl.ANY)
HBM = pl.BlockSpec(memory_space=pltpu.HBM)


def iota(shape, dim):
    return lax.broadcasted_iota(jnp.int32, shape, dim)


def weights_kernel(places_ref, stem_ref, mw_ref, w4_ref, mid_ref):
    for n in range(8):
        part = places_ref[384 * n : 384 * n + 384, :]
        w4_ref[n] = jnp.dot(part, stem_ref[...], preferred_element_type=F32).astype(BF16)
    for k in range(9):
        g0, g1, g2 = (
            mw_ref[384 * k + 128 * c : 384 * k + 128 * c + 128].astype(F32) for c in range(3)
        )
        outer = (g0 + g2) * 0.5
        inner = g1 * 0.5
        mid_ref[0, 128 * k : 128 * k + 128] = (outer + inner).astype(BF16)
        mid_ref[1, 128 * k : 128 * k + 128] = (outer - inner).astype(BF16)


def fetch_kernel(keep, train, fr, keep_out, train_out, fr_out, sems):
    pairs = ((keep, keep_out), (train, train_out), (fr, fr_out))
    copies = [pltpu.make_async_copy(src, dst, sems.at[i]) for i, (src, dst) in enumerate(pairs)]
    for copy in copies:
        copy.start()
    for copy in copies:
        copy.wait()


def pack_kernel(core_ref, keep_s, keep_t, train_s, fra, frb, out_ref):
    out_ref[...] = jnp.zeros_like(out_ref)
    core = core_ref[0]
    for keep_ref, fr in ((keep_s, fra), (keep_t, frb)):
        for j in range(fr.shape[0]):
            k = keep_ref[j]
            t = train_s[jnp.maximum(k, 0)]
            mine = jnp.logical_and(k >= 0, ((t >> 2) & 1) == core)

            @pl.when(mine)
            def _():
                out_ref[t >> 3, t & 3] = fr[j]


def combine_kernel(recv_ref, out_ref, rows_ref):
    for k in range(4):
        for ch in range(3):
            total = recv_ref[0, k, ch].astype(F32)
            for s in range(1, recv_ref.shape[0]):
                total = total + recv_ref[s, k, ch].astype(F32)
            at = (k * 3 + ch) * 4
            rows_ref[at : at + 4, :] = total
    i = iota((256, 256), 0)
    o = iota((256, 256), 1)
    source = ((o >> 5) & 3) * 64 + (o & 31) * 2 + (o >> 7)
    pick = (i == source).astype(F32).astype(BF16)
    split = jnp.dot(rows_ref[...].astype(BF16), pick, preferred_element_type=F32)
    rows_ref[...] = split
    for k in range(4):
        for ch in range(3):
            at = (k * 3 + ch) * 4
            piece = rows_ref[at : at + 4, :].astype(BF16)
            for y in range(4):
                out_ref[y * 4 + k, ch] = piece


def group_scale(total, square, cells, per_group, gain, shift):
    n = total.shape[1]
    gi = iota((n, n), 0) // per_group
    gj = iota((n, n), 1) // per_group
    member = (gi == gj).astype(F32)
    both = jnp.concatenate([total, square, jnp.zeros((6, n), F32)], axis=0)
    sums = jnp.dot(both, member, precision=lax.Precision.HIGHEST, preferred_element_type=F32)
    sums = sums * (1.0 / (cells * per_group))
    mean = sums[0:1]
    spread = sums[1:2] - mean * mean
    scale = gain * lax.rsqrt(spread + eps)
    return scale, shift - mean * scale


def silu(u):
    half = 0.5 * u
    return half + half * jnp.tanh(half)


def mixer_kernel(
    y_ref,
    raw_ref,
    w4_hbm,
    gain_hbm,
    shift_hbm,
    mw_ref,
    mid_ref,
    mix_ref,
    stat_ref,
    dv,
    tg,
    stem,
    hid,
    w4_ref,
    gain_ref,
    shift_ref,
    sems,
):
    y = y_ref[0]
    copies = [
        pltpu.make_async_copy(gain_hbm, gain_ref, sems.at[0]),
        pltpu.make_async_copy(shift_hbm, shift_ref, sems.at[1]),
        pltpu.make_async_copy(w4_hbm, w4_ref, sems.at[2]),
    ]
    for copy in copies:
        copy.start()
    for yy in range(4):
        for xx in range(4):
            for ch in range(3):
                piece = raw_ref[yy * 4 + xx, ch].astype(F32)
                for par in range(2):
                    dv[1 + par, ch, 4 + 4 * xx : 8 + 4 * xx, 128 * yy : 128 * yy + 128] = piece[
                        :, 128 * par : 128 * par + 128
                    ]
    pair = iota((16, 512), 1) & 31
    for ch in range(3):
        even = dv[1, ch, 4:20, :]
        odd = dv[2, ch, 4:20, :]
        dv[0, ch, 4:20, :] = jnp.where(pair == 0, 0.0, pltpu.roll(odd, 1, 1))
        dv[3, ch, 4:20, :] = jnp.where(pair == 31, 0.0, pltpu.roll(even, 511, 1))
    for v in range(4):
        for ch in range(3):
            dv[v, ch, 0:4, :] = jnp.broadcast_to(dv[v, ch, 4:5, :], (4, 512))
    edge = jnp.zeros((32, 128), BF16)
    for g in range(4):
        tg[g, 0:32, :] = edge
        tg[g, 544:576, :] = edge
        rows = [dv[v, ch, 4 * g : 4 * g + 8, :] for v in range(4) for ch in range(3)]
        block = jnp.concatenate(rows + [jnp.zeros((32, 512), F32)], axis=0)
        tg[g, 32:544, :] = jnp.transpose(block).astype(BF16)
    for copy in copies:
        copy.wait()
    total = jnp.zeros((8, 1024), F32)
    square = jnp.zeros((8, 1024), F32)
    for g in range(4):
        stem[g, 0:32, :] = jnp.zeros((32, 1024), F32)
        stem[g, 544:576, :] = jnp.zeros((32, 1024), F32)
        left = jnp.concatenate([tg[g, 32 * b : 32 * b + 512, :] for b in range(3)], axis=1)
        w4 = jnp.concatenate([w4_ref[n] for n in range(8)], axis=1)
        out = jnp.dot(left, w4, preferred_element_type=F32)
        stem[g, 32:544, :] = out
        parts = out.reshape(64, 8, 1024)
        total = total + jnp.sum(parts, axis=0)
        square = square + jnp.sum(parts * parts, axis=0)
    total = jnp.sum(total, axis=0, keepdims=True)
    square = jnp.sum(square, axis=0, keepdims=True)
    total = sum(total[:, 128 * k : 128 * k + 128] for k in range(8))
    square = sum(square[:, 128 * k : 128 * k + 128] for k in range(8))
    scale, offset = group_scale(total, square, 16384, 4, gain_ref[...], shift_ref[...])
    at = iota((192, 128), 0)
    row = at >> 5
    valid = jnp.logical_and(
        jnp.logical_or(row > 0, y > 0), jnp.logical_or(row < 5, y < 3)
    )
    first = (at & 31) == 0
    last = (at & 31) == 31
    start = pl.multiple_of(y * 128, 128)
    for f in range(16):
        g, fo = divmod(f, 4)
        val = stem[g, pl.ds(start, 192), 256 * fo : 256 * fo + 256]
        even = jnp.where(valid, silu(val[:, :128] * scale + offset), 0.0)
        odd = jnp.where(valid, silu(val[:, 128:] * scale + offset), 0.0)
        before = jnp.where(first, 0.0, pltpu.roll(odd, 1, 0))
        after = jnp.where(last, 0.0, pltpu.roll(even, 191, 0))
        parts = (before - odd, even + odd, odd - even, even - after)
        for k, part in enumerate(parts):
            part = part.astype(BF16)
            hid[f + 2, :, 128 * k : 128 * k + 128] = part
            if f == 0:
                hid[0, :, 128 * k : 128 * k + 128] = part
                hid[1, :, 128 * k : 128 * k + 128] = part

    s = jnp.zeros((8, 256), F32)
    q = jnp.zeros((8, 256), F32)
    steps = [(a, b) for a in range(3) for b in range(3)]
    first_tap = [mw_ref[384 * k : 384 * k + 128] for k in range(9)]
    last_tap = [mw_ref[384 * k + 256 : 384 * k + 384] for k in range(9)]
    weights = (
        jnp.concatenate(first_tap[:8], axis=0),
        mid_ref[0, :1024],
        mid_ref[1, :1024],
        jnp.concatenate(last_tap[:8], axis=0),
    )
    tail_even = jnp.concatenate([first_tap[8], mid_ref[0, 1024:]], axis=0)
    tail_odd = jnp.concatenate([mid_ref[0, 1024:], -last_tap[8]], axis=0)
    tail_both = mid_ref[1, 1024:]
    for f in range(0, 16, 4):

        def tap(k, a, b):
            cut = hid[f + a : f + a + 4, 32 * b : 32 * b + 128, 128 * k : 128 * k + 128]
            return cut.reshape(512, 128)

        m = []
        for k in range(4):
            left = jnp.concatenate([tap(k, a, b) for a, b in steps[:8]], axis=1)
            m.append(jnp.dot(left, weights[k], preferred_element_type=F32))
        t = [tap(k, 2, 2) for k in range(4)]
        even = jnp.dot(jnp.concatenate([t[0], t[1]], axis=1), tail_even, preferred_element_type=F32)
        odd = jnp.dot(jnp.concatenate([t[1], t[3]], axis=1), tail_odd, preferred_element_type=F32)
        both = jnp.dot(t[2], tail_both, preferred_element_type=F32) + m[2]
        even = even + m[0] + (m[1] + both)
        odd = odd - m[3] + (m[1] - both)
        for par, out in enumerate((even, odd)):
            mix_ref[par, f : f + 4] = out.reshape(4, 128, 256)
            parts = out.reshape(64, 8, 256)
            s = s + jnp.sum(parts, axis=0)
            q = q + jnp.sum(parts * parts, axis=0)
    stat_ref[0:1, :] = jnp.sum(s, axis=0, keepdims=True)
    stat_ref[1:2, :] = jnp.sum(q, axis=0, keepdims=True)


def down_kernel(mix_ref, stat_a, stat_b, stat_c, stat_d, gain_ref, shift_ref, dw_ref, bias_ref, out_ref, left):
    stat = (stat_a[...] + stat_b[...]) + (stat_c[...] + stat_d[...])
    scale, offset = group_scale(
        stat[0:1, :], stat[1:2, :], 16384, 8, gain_ref[...], shift_ref[...]
    )
    for g in range(8):
        for par in range(2):
            one = silu(mix_ref[par, 2 * g] * scale + offset)
            two = silu(mix_ref[par, 2 * g + 1] * scale + offset)
            pooled = ((one + two) * 0.5).astype(BF16)
            for r in range(4):
                lane = ((r & 1) * 2 + par) * 256
                to = g * 64 + (r >> 1) * 32
                left[to : to + 32, lane : lane + 256] = pooled[32 * r : 32 * r + 32]
    out = jnp.dot(left[...], dw_ref[...], preferred_element_type=F32) + bias_ref[...]
    out_ref[...] = out.astype(BF16)


def stem_places():
    place = np.zeros((8, 3, 128, 81), np.float32)
    for fo in range(4):
        for par in range(2):
            for a in range(3):
                for b in range(3):
                    for c in range(3):
                        for ch in range(3):
                            row = (par + c) * 24 + ch * 8 + fo + 2 + a
                            place[fo * 2 + par, b, row, ((a * 3 + b) * 3 + c) * 3 + ch] = 1
    return place.reshape(3072, 81)


def in_hbm(array):
    return pltpu.with_memory_space_constraint(array, pltpu.HBM)


def call(kernel, out_shape, specs, scratch=(), mib=16):
    return pl.pallas_call(
        kernel,
        out_shape=out_shape,
        in_specs=specs,
        out_specs=jax.tree.map(lambda _: VMEM, out_shape),
        scratch_shapes=list(scratch),
        compiler_params=pltpu.CompilerParams(vmem_limit_bytes=mib << 20),
    )


def local(
    frames,
    keep_list,
    train_slot,
    stem_weight,
    stem_gain,
    stem_shift,
    mixer_weight,
    mixer_gain,
    mixer_shift,
    down_weight,
    down_bias,
):
    sds = jax.ShapeDtypeStruct
    index = lax.axis_index("clip")
    core = (index % 2).astype(jnp.int32).reshape(1)
    row = lax.axis_index("row").astype(jnp.int32).reshape(1)
    pairs = [(i, i ^ 1) for i in range(16)]
    frames_b = lax.ppermute(frames, "clip", pairs)
    keep_b = lax.ppermute(keep_list, "clip", pairs)
    keep_a, train, frames_a = call(
        fetch_kernel,
        (sds((8,), jnp.int32), sds((64,), jnp.int32), sds((8, 3, 4, 256), BF16)),
        [HBM] * 3,
        [pltpu.SemaphoreType.DMA((3,))],
    )(in_hbm(keep_list), in_hbm(train_slot), in_hbm(frames))
    packed = call(
        pack_kernel, sds((8, 4, 3, 4, 256), BF16), [SMEM] * 4 + [VMEM] * 2
    )(core, keep_a, keep_b, train, frames_a, frames_b)
    places = jnp.asarray(stem_places(), BF16)
    packed, mixer_weight = lax.optimization_barrier((packed, mixer_weight.reshape(3456, 256)))
    w4, middle = call(
        weights_kernel,
        (sds((8, 384, 128), BF16), sds((2, 1152, 256), BF16)),
        [VMEM] * 3,
    )(places, stem_weight, mixer_weight)
    along_z = [[2 * z + k for z in range(8)] for k in range(2)]
    received = lax.all_to_all(
        packed, "clip", split_axis=0, concat_axis=0, tiled=True, axis_index_groups=along_z
    )
    pieces = call(
        combine_kernel, sds((16, 3, 4, 256), BF16), [VMEM], [pltpu.VMEM((48, 256), F32)]
    )(received)
    pieces, w4, middle = lax.optimization_barrier((pieces, w4, middle))
    raw = lax.all_to_all(pieces, ("row", "tm"), split_axis=0, concat_axis=0, tiled=True)
    mix, stat = call(
        mixer_kernel,
        (sds((2, 16, 128, 256), F32), sds((2, 256), F32)),
        [SMEM, VMEM, HBM, HBM, HBM, VMEM, VMEM],
        [
            pltpu.VMEM((4, 3, 24, 512), F32),
            pltpu.VMEM((4, 576, 128), BF16),
            pltpu.VMEM((4, 576, 1024), F32),
            pltpu.VMEM((18, 192, 512), BF16),
            pltpu.VMEM((8, 384, 128), BF16),
            pltpu.VMEM((1, 128), F32),
            pltpu.VMEM((1, 128), F32),
            pltpu.SemaphoreType.DMA((3,)),
        ],
        mib=24,
    )(
        row,
        raw,
        in_hbm(w4),
        in_hbm(stem_gain.reshape(1, -1)),
        in_hbm(stem_shift.reshape(1, -1)),
        mixer_weight,
        middle,
    )
    others = [
        lax.ppermute(stat, "row", [(i, (i + by) % 4) for i in range(4)]) for by in (1, 2, 3)
    ]
    latent = call(
        down_kernel, sds((512, 256), BF16), [VMEM] * 9, [pltpu.VMEM((512, 1024), BF16)], mib=16
    )(
        mix,
        stat,
        *others,
        mixer_gain.reshape(1, -1),
        mixer_shift.reshape(1, -1),
        down_weight,
        down_bias.reshape(1, -1),
    )
    return lax.all_to_all(
        latent.reshape(4, 2, 2, 32, 256), "tm", split_axis=0, concat_axis=0, tiled=True
    )


def solution(mesh):
    return jax.shard_map(
        local,
        mesh=mesh,
        in_specs=(P("clip", None, "tm", "row"), P("clip")) + (P(),) * 9,
        out_specs=P("clip", "tm", "row", None, None),
        check_vma=False,
    )
```

```python
import jax
import jax.numpy as jnp
import numpy as np
from jax import lax
from jax.experimental import pallas as pl
from jax.experimental.pallas import tpu as pltpu
from jax.sharding import PartitionSpec as P

GROUPS = 32
COLS = 64
F32 = jnp.float32
BF16 = jnp.bfloat16
eps = 1e-06

VMEM = pl.BlockSpec(memory_space=pltpu.VMEM)
SMEM = pl.BlockSpec(memory_space=pltpu.SMEM)
ANY = pl.BlockSpec(memory_space=pl.ANY)
HBM = pl.BlockSpec(memory_space=pltpu.HBM)


def iota(shape, dim):
    return lax.broadcasted_iota(jnp.int32, shape, dim)


def weights_kernel(places_hbm, stem_hbm, mw_hbm, w4_ref, taps_ref, places, stem, mw, sems):
    pairs = ((places_hbm, places), (stem_hbm, stem), (mw_hbm, mw))
    copies = [pltpu.make_async_copy(src, dst, sems.at[i]) for i, (src, dst) in enumerate(pairs)]
    for copy in copies:
        copy.start()
    copies[0].wait()
    copies[1].wait()
    for n in range(8):
        part = places[256 * n : 256 * n + 256, :]
        w4_ref[n] = jnp.dot(part, stem[...], preferred_element_type=F32).astype(BF16)
    copies[2].wait()
    for k in range(9):
        g0, g1, g2 = (mw[384 * k + 128 * c : 384 * k + 128 * c + 128] for c in range(3))
        outer = (g0.astype(F32) + g2.astype(F32)) * 0.5
        inner = g1.astype(F32) * 0.5
        at = slice(128 * k, 128 * k + 128)
        taps_ref[0, at] = g0
        taps_ref[1, at] = (outer + inner).astype(BF16)
        taps_ref[2, at] = (outer - inner).astype(BF16)
        taps_ref[3, at] = g2


def fetch_kernel(keep, train, fr, keep_out, train_out, fr_out, sems):
    pairs = ((keep, keep_out), (train, train_out), (fr, fr_out))
    copies = [pltpu.make_async_copy(src, dst, sems.at[i]) for i, (src, dst) in enumerate(pairs)]
    for copy in copies:
        copy.start()
    for copy in copies:
        copy.wait()


def pack_kernel(core_ref, keep_s, keep_t, train_s, fra, frb, out_ref):
    out_ref[...] = jnp.zeros_like(out_ref)
    core = core_ref[0]
    for keep_ref, fr in ((keep_s, fra), (keep_t, frb)):
        for j in range(fr.shape[0]):
            k = keep_ref[j]
            t = train_s[jnp.maximum(k, 0)]
            mine = jnp.logical_and(k >= 0, ((t >> 2) & 1) == core)

            @pl.when(mine)
            def _():
                out_ref[t >> 3, t & 3] = fr[j]


def combine_kernel(recv_ref, out_ref, rows_ref):
    for k in range(4):
        for ch in range(3):
            total = recv_ref[0, k, ch].astype(F32)
            for s in range(1, recv_ref.shape[0]):
                total = total + recv_ref[s, k, ch].astype(F32)
            at = (k * 3 + ch) * 4
            rows_ref[at : at + 4, :] = total
    i = iota((256, 256), 0)
    o = iota((256, 256), 1)
    source = ((o >> 5) & 3) * 64 + (o & 31) * 2 + (o >> 7)
    pick = (i == source).astype(F32).astype(BF16)
    split = jnp.dot(rows_ref[...].astype(BF16), pick, preferred_element_type=F32)
    rows_ref[...] = split
    for k in range(4):
        for ch in range(3):
            at = (k * 3 + ch) * 4
            piece = rows_ref[at : at + 4, :].astype(BF16)
            for y in range(4):
                out_ref[y * 4 + k, ch] = piece


def group_scale(total, square, cells, per_group, gain, shift):
    n = total.shape[1]
    gi = iota((n, n), 0) // per_group
    gj = iota((n, n), 1) // per_group
    member = (gi == gj).astype(F32)
    both = jnp.concatenate([total, square, jnp.zeros((6, n), F32)], axis=0)
    sums = jnp.dot(both, member, precision=lax.Precision.HIGHEST, preferred_element_type=F32)
    sums = sums * (1.0 / (cells * per_group))
    mean = sums[0:1]
    spread = sums[1:2] - mean * mean
    scale = gain * lax.rsqrt(spread + eps)
    return scale, shift - mean * scale


def silu(u):
    half = 0.5 * u
    return half + half * jnp.tanh(half)


def mixer_kernel(
    y_ref,
    raw_ref,
    w4_ref,
    gain_hbm,
    shift_hbm,
    taps_ref,
    mix_ref,
    stat_ref,
    dv,
    rows,
    tg,
    stem,
    hid,
    gain_ref,
    shift_ref,
    sems,
):
    y = y_ref[0]
    copies = [
        pltpu.make_async_copy(gain_hbm, gain_ref, sems.at[0]),
        pltpu.make_async_copy(shift_hbm, shift_ref, sems.at[1]),
    ]
    for copy in copies:
        copy.start()
    for yy in range(4):
        for xx in range(4):
            for ch in range(3):
                piece = raw_ref[yy * 4 + xx, ch].astype(F32)
                for par in range(2):
                    dv[par, ch, 4 * xx : 4 * xx + 4, 128 * yy : 128 * yy + 128] = piece[
                        :, 128 * par : 128 * par + 128
                    ]
    lane = iota((16, 512), 1)
    pair = lane & 31
    for ch in range(3):
        even = dv[0, ch]
        odd = dv[1, ch]
        before = jnp.where(pair == 0, 0.0, pltpu.roll(odd, 1, 1))
        after = jnp.where(pair == 31, 0.0, pltpu.roll(even, 511, 1))
        for v, plane in enumerate((before, even, odd, after)):
            above = jnp.where(lane < 32, 0.0, pltpu.roll(plane, 32, 1))
            below = jnp.where(lane >= 480, 0.0, pltpu.roll(plane, 480, 1))
            at = v * 3 + ch
            for b, part in enumerate((above, plane, below)):
                for j in range(4):
                    cut = part[:, 128 * j : 128 * j + 128]
                    rows[b, j, pl.ds(24 + at, 16, stride=12), :] = cut
                    rows[b, j, at : at + 1, :] = cut[0:1]
                    rows[b, j, 12 + at : 13 + at, :] = cut[0:1]
    for g in range(4):
        for j in range(4):
            taps = [rows[b, j, 48 * g : 48 * g + 72, :] for b in range(3)]
            block = jnp.concatenate(taps + [jnp.zeros((40, 128), F32)], axis=0)
            tg[g, 128 * j : 128 * j + 128, :] = jnp.transpose(block).astype(BF16)
    total = jnp.zeros((8, 1024), F32)
    square = jnp.zeros((8, 1024), F32)
    for g in range(4):
        stem[g, 0:32, :] = jnp.zeros((32, 1024), F32)
        stem[g, 544:576, :] = jnp.zeros((32, 1024), F32)
        w4 = jnp.concatenate([w4_ref[n] for n in range(8)], axis=1)
        out = jnp.dot(tg[g], w4, preferred_element_type=F32)
        stem[g, 32:544, :] = out
        parts = out.reshape(64, 8, 1024)
        total = total + jnp.sum(parts, axis=0)
        square = square + jnp.sum(parts * parts, axis=0)
    total = jnp.sum(total, axis=0, keepdims=True)
    square = jnp.sum(square, axis=0, keepdims=True)
    total = sum(total[:, 128 * k : 128 * k + 128] for k in range(8))
    square = sum(square[:, 128 * k : 128 * k + 128] for k in range(8))
    for copy in copies:
        copy.wait()
    scale, offset = group_scale(total, square, 16384, 4, gain_ref[...], shift_ref[...])
    at = iota((192, 128), 0)
    first = (at & 31) == 0
    last = (at & 31) == 31
    start = pl.multiple_of(y * 128, 128)
    top = jnp.where(y > 0, 1.0, 0.0)
    bottom = jnp.where(y < 3, 1.0, 0.0)
    scale = scale * 0.5
    offset = offset * 0.5

    def act(val):
        half = val * scale + offset
        out = half + half * jnp.tanh(half)
        return jnp.concatenate([out[:32] * top, out[32:160], out[160:] * bottom], axis=0)

    def make_hidden(f):
        g, fo = divmod(f, 4)
        val = stem[g, pl.ds(start, 192), 256 * fo : 256 * fo + 256]
        even = act(val[:, :128])
        odd = act(val[:, 128:])
        before = jnp.where(first, 0.0, pltpu.roll(odd, 1, 0))
        after = jnp.where(last, 0.0, pltpu.roll(even, 191, 0))
        parts = (before - odd, even + odd, odd - even, even - after)
        for k, part in enumerate(parts):
            part = part.astype(BF16)
            hid[f + 2, :, 128 * k : 128 * k + 128] = part
            if f == 0:
                hid[0, :, 128 * k : 128 * k + 128] = part
                hid[1, :, 128 * k : 128 * k + 128] = part

    s = jnp.zeros((8, 256), F32)
    q = jnp.zeros((8, 256), F32)
    steps = [(a, b) for a in range(3) for b in range(3)]
    tail_even = jnp.concatenate([taps_ref[0, 1024:], taps_ref[1, 1024:]], axis=0)
    tail_odd = jnp.concatenate([taps_ref[1, 1024:], -taps_ref[3, 1024:]], axis=0)
    tail_both = taps_ref[2, 1024:]
    for k in range(16):
        make_hidden(k)
    for f in range(0, 16, 4):

        def tap(k, a, b):
            cut = hid[f + a : f + a + 4, 32 * b : 32 * b + 128, 128 * k : 128 * k + 128]
            return cut.reshape(512, 128)

        m = []
        for k in range(4):
            left = jnp.concatenate([tap(k, a, b) for a, b in steps[:8]], axis=1)
            m.append(jnp.dot(left, taps_ref[k, :1024], preferred_element_type=F32))
        t = [tap(k, 2, 2) for k in range(4)]
        even = jnp.dot(jnp.concatenate([t[0], t[1]], axis=1), tail_even, preferred_element_type=F32)
        odd = jnp.dot(jnp.concatenate([t[1], t[3]], axis=1), tail_odd, preferred_element_type=F32)
        both = jnp.dot(t[2], tail_both, preferred_element_type=F32) + m[2]
        even = even + m[0] + (m[1] + both)
        odd = odd - m[3] + (m[1] - both)
        for par, out in enumerate((even, odd)):
            mix_ref[par, f : f + 4] = out.reshape(4, 128, 256)
            parts = out.reshape(64, 8, 256)
            s = s + jnp.sum(parts, axis=0)
            q = q + jnp.sum(parts * parts, axis=0)
    stat_ref[0:1, :] = jnp.sum(s, axis=0, keepdims=True)
    stat_ref[1:2, :] = jnp.sum(q, axis=0, keepdims=True)


def down_kernel(mix_ref, stat_a, stat_b, stat_c, stat_d, gain_ref, shift_ref, dw_ref, bias_ref, out_ref, left):
    stat = (stat_a[...] + stat_b[...]) + (stat_c[...] + stat_d[...])
    scale, offset = group_scale(
        stat[0:1, :], stat[1:2, :], 16384, 8, gain_ref[...], shift_ref[...]
    )
    for g in range(8):
        for par in range(2):
            one = silu(mix_ref[par, 2 * g] * scale + offset)
            two = silu(mix_ref[par, 2 * g + 1] * scale + offset)
            pooled = ((one + two) * 0.5).astype(BF16)
            for r in range(4):
                lane = ((r & 1) * 2 + par) * 256
                to = g * 64 + (r >> 1) * 32
                left[to : to + 32, lane : lane + 256] = pooled[32 * r : 32 * r + 32]
    out = jnp.dot(left[...], dw_ref[...], preferred_element_type=F32) + bias_ref[...]
    out_ref[...] = out.astype(BF16)


def stem_places():
    place = np.zeros((8, 256, 81), np.float32)
    for fo in range(4):
        for par in range(2):
            for a in range(3):
                for b in range(3):
                    for c in range(3):
                        for ch in range(3):
                            row = b * 72 + (fo + a) * 12 + (par + c) * 3 + ch
                            place[fo * 2 + par, row, ((a * 3 + b) * 3 + c) * 3 + ch] = 1
    return place.reshape(2048, 81)


def in_hbm(array):
    return pltpu.with_memory_space_constraint(array, pltpu.HBM)


def call(kernel, out_shape, specs, scratch=(), mib=16):
    return pl.pallas_call(
        kernel,
        out_shape=out_shape,
        in_specs=specs,
        out_specs=jax.tree.map(lambda _: VMEM, out_shape),
        scratch_shapes=list(scratch),
        compiler_params=pltpu.CompilerParams(vmem_limit_bytes=mib << 20),
    )


def local(
    frames,
    keep_list,
    train_slot,
    stem_weight,
    stem_gain,
    stem_shift,
    mixer_weight,
    mixer_gain,
    mixer_shift,
    down_weight,
    down_bias,
):
    sds = jax.ShapeDtypeStruct
    index = lax.axis_index("clip")
    core = (index % 2).astype(jnp.int32).reshape(1)
    row = lax.axis_index("row").astype(jnp.int32).reshape(1)
    pairs = [(i, i ^ 1) for i in range(16)]
    frames_b = lax.ppermute(frames, "clip", pairs)
    keep_b = lax.ppermute(keep_list, "clip", pairs)
    keep_a, train, frames_a = call(
        fetch_kernel,
        (sds((8,), jnp.int32), sds((64,), jnp.int32), sds((8, 3, 4, 256), BF16)),
        [HBM] * 3,
        [pltpu.SemaphoreType.DMA((3,))],
    )(in_hbm(keep_list), in_hbm(train_slot), in_hbm(frames))
    packed = call(
        pack_kernel, sds((8, 4, 3, 4, 256), BF16), [SMEM] * 4 + [VMEM] * 2
    )(core, keep_a, keep_b, train, frames_a, frames_b)
    along_z = [[2 * z + k for z in range(8)] for k in range(2)]
    received = lax.all_to_all(
        packed, "clip", split_axis=0, concat_axis=0, tiled=True, axis_index_groups=along_z
    )
    pieces = call(
        combine_kernel, sds((16, 3, 4, 256), BF16), [VMEM], [pltpu.VMEM((48, 256), F32)]
    )(received)
    places = jnp.asarray(stem_places(), BF16)
    pieces, places = lax.optimization_barrier((pieces, places))
    w4, taps = call(
        weights_kernel,
        (sds((8, 256, 128), BF16), sds((4, 1152, 256), BF16)),
        [HBM] * 3,
        [
            pltpu.VMEM((2048, 81), BF16),
            pltpu.VMEM((81, 128), BF16),
            pltpu.VMEM((3456, 256), BF16),
            pltpu.SemaphoreType.DMA((3,)),
        ],
    )(in_hbm(places), in_hbm(stem_weight), in_hbm(mixer_weight.reshape(3456, 256)))
    raw = lax.all_to_all(pieces, ("row", "tm"), split_axis=0, concat_axis=0, tiled=True)
    mix, stat = call(
        mixer_kernel,
        (sds((2, 16, 128, 256), F32), sds((2, 256), F32)),
        [SMEM, VMEM, VMEM, HBM, HBM, VMEM],
        [
            pltpu.VMEM((2, 3, 16, 512), F32),
            pltpu.VMEM((3, 4, 216, 128), F32),
            pltpu.VMEM((4, 512, 256), BF16),
            pltpu.VMEM((4, 576, 1024), F32),
            pltpu.VMEM((18, 192, 512), BF16),
            pltpu.VMEM((1, 128), F32),
            pltpu.VMEM((1, 128), F32),
            pltpu.SemaphoreType.DMA((2,)),
        ],
        mib=24,
    )(
        row,
        raw,
        w4,
        in_hbm(stem_gain.reshape(1, -1)),
        in_hbm(stem_shift.reshape(1, -1)),
        taps,
    )
    others = [
        lax.ppermute(stat, "row", [(i, (i + by) % 4) for i in range(4)]) for by in (1, 2, 3)
    ]
    latent = call(
        down_kernel, sds((512, 256), BF16), [VMEM] * 9, [pltpu.VMEM((512, 1024), BF16)], mib=16
    )(
        mix,
        stat,
        *others,
        mixer_gain.reshape(1, -1),
        mixer_shift.reshape(1, -1),
        down_weight,
        down_bias.reshape(1, -1),
    )
    return lax.all_to_all(
        latent.reshape(4, 2, 2, 32, 256), "tm", split_axis=0, concat_axis=0, tiled=True
    )


def solution(mesh):
    return jax.shard_map(
        local,
        mesh=mesh,
        in_specs=(P("clip", None, "tm", "row"), P("clip")) + (P(),) * 9,
        out_specs=P("clip", "tm", "row", None, None),
        check_vma=False,
    )
```

```python
import functools

import jax
import jax.numpy as jnp
import numpy as np
from jax import lax
from jax.experimental import pallas as pl
from jax.experimental.pallas import tpu as pltpu
from jax.sharding import PartitionSpec as P

F32 = jnp.float32
BF16 = jnp.bfloat16
eps = 1e-06

VMEM = pl.BlockSpec(memory_space=pltpu.VMEM)
SMEM = pl.BlockSpec(memory_space=pltpu.SMEM)
ANY = pl.BlockSpec(memory_space=pl.ANY)
HBM = pl.BlockSpec(memory_space=pltpu.HBM)


def iota(shape, dim):
    return lax.broadcasted_iota(jnp.int32, shape, dim)


def weights_kernel(places_hbm, stem_hbm, mw_hbm, w4_ref, taps_ref, places, stem, mw, sems):
    pairs = ((places_hbm, places), (stem_hbm, stem), (mw_hbm, mw))
    copies = [pltpu.make_async_copy(src, dst, sems.at[i]) for i, (src, dst) in enumerate(pairs)]
    for copy in copies:
        copy.start()
    copies[0].wait()
    copies[1].wait()
    for n in range(8):
        part = places[256 * n : 256 * n + 256, :]
        w4_ref[n] = jnp.dot(part, stem[...], preferred_element_type=F32).astype(BF16)
    copies[2].wait()
    for k in range(9):
        g0, g1, g2 = (mw[384 * k + 128 * c : 384 * k + 128 * c + 128] for c in range(3))
        outer = (g0.astype(F32) + g2.astype(F32)) * 0.5
        inner = g1.astype(F32) * 0.5
        at = slice(128 * k, 128 * k + 128)
        taps_ref[0, at] = g0
        taps_ref[1, at] = (outer + inner).astype(BF16)
        taps_ref[2, at] = (outer - inner).astype(BF16)
        taps_ref[3, at] = g2


def fetch_kernel(keep, train, fr, keep_out, train_out, fr_out, sems):
    pairs = ((keep, keep_out), (train, train_out), (fr, fr_out))
    copies = [pltpu.make_async_copy(src, dst, sems.at[i]) for i, (src, dst) in enumerate(pairs)]
    for copy in copies:
        copy.start()
    for copy in copies:
        copy.wait()


def pack_kernel(core_ref, keep_s, keep_t, train_s, fra, frb, out_ref):
    out_ref[...] = jnp.zeros_like(out_ref)
    core = core_ref[0]
    for keep_ref, fr in ((keep_s, fra), (keep_t, frb)):
        for j in range(fr.shape[0]):
            k = keep_ref[j]
            t = train_s[jnp.maximum(k, 0)]
            mine = jnp.logical_and(k >= 0, ((t >> 2) & 1) == core)

            @pl.when(mine)
            def _():
                out_ref[t >> 3, t & 3] = fr[j]


def combine_kernel(recv_ref, out_ref, rows_ref):
    for k in range(4):
        for ch in range(3):
            total = recv_ref[0, k, ch].astype(F32)
            for s in range(1, recv_ref.shape[0]):
                total = total + recv_ref[s, k, ch].astype(F32)
            at = (k * 3 + ch) * 4
            rows_ref[at : at + 4, :] = total
    i = iota((256, 256), 0)
    o = iota((256, 256), 1)
    source = ((o >> 5) & 3) * 64 + (o & 31) * 2 + (o >> 7)
    pick = (i == source).astype(F32).astype(BF16)
    split = jnp.dot(rows_ref[...].astype(BF16), pick, preferred_element_type=F32)
    rows_ref[...] = split
    for k in range(4):
        for ch in range(3):
            at = (k * 3 + ch) * 4
            piece = rows_ref[at : at + 4, :].astype(BF16)
            for y in range(4):
                out_ref[y * 4 + k, ch] = piece


def group_scale(total, square, cells, per_group, gain, shift):
    n = total.shape[1]
    gi = iota((n, n), 0) // per_group
    gj = iota((n, n), 1) // per_group
    member = (gi == gj).astype(F32)
    both = jnp.concatenate([total, square, jnp.zeros((6, n), F32)], axis=0)
    sums = jnp.dot(both, member, precision=lax.Precision.HIGHEST, preferred_element_type=F32)
    sums = sums * (1.0 / (cells * per_group))
    mean = sums[0:1]
    spread = sums[1:2] - mean * mean
    scale = gain * lax.rsqrt(spread + eps)
    return scale, shift - mean * scale


def mixer_kernel(
    y_ref,
    raw_ref,
    w4_ref,
    gain_hbm,
    shift_hbm,
    taps_ref,
    mix_ref,
    stat_ref,
    dv,
    rows,
    tg,
    stem,
    hid,
    gain_ref,
    shift_ref,
    sems,
):
    y = y_ref[0]
    copies = [
        pltpu.make_async_copy(gain_hbm, gain_ref, sems.at[0]),
        pltpu.make_async_copy(shift_hbm, shift_ref, sems.at[1]),
    ]
    for copy in copies:
        copy.start()
    for yy in range(4):
        for xx in range(4):
            for ch in range(3):
                piece = raw_ref[yy * 4 + xx, ch].astype(F32)
                for par in range(2):
                    dv[par, ch, 4 * xx : 4 * xx + 4, 128 * yy : 128 * yy + 128] = piece[
                        :, 128 * par : 128 * par + 128
                    ]
    lane = iota((16, 512), 1)
    pair = lane & 31
    for ch in range(3):
        even = dv[0, ch]
        odd = dv[1, ch]
        before = jnp.where(pair == 0, 0.0, pltpu.roll(odd, 1, 1))
        after = jnp.where(pair == 31, 0.0, pltpu.roll(even, 511, 1))
        for v, plane in enumerate((before, even, odd, after)):
            above = jnp.where(lane < 32, 0.0, pltpu.roll(plane, 32, 1))
            below = jnp.where(lane >= 480, 0.0, pltpu.roll(plane, 480, 1))
            at = v * 3 + ch
            for b, part in enumerate((above, plane, below)):
                for j in range(4):
                    cut = part[:, 128 * j : 128 * j + 128]
                    rows[b, j, pl.ds(24 + at, 16, stride=12), :] = cut
                    rows[b, j, at : at + 1, :] = cut[0:1]
                    rows[b, j, 12 + at : 13 + at, :] = cut[0:1]
    for g in range(4):
        for j in range(4):
            taps = [rows[b, j, 48 * g : 48 * g + 72, :] for b in range(3)]
            block = jnp.concatenate(taps + [jnp.zeros((40, 128), F32)], axis=0)
            tg[g, 128 * j : 128 * j + 128, :] = jnp.transpose(block).astype(BF16)
    total = jnp.zeros((8, 1024), F32)
    square = jnp.zeros((8, 1024), F32)
    for g in range(4):
        stem[g, 0:32, :] = jnp.zeros((32, 1024), F32)
        stem[g, 544:576, :] = jnp.zeros((32, 1024), F32)
        w4 = jnp.concatenate([w4_ref[n] for n in range(8)], axis=1)
        out = jnp.dot(tg[g], w4, preferred_element_type=F32)
        stem[g, 32:544, :] = out
        parts = out.reshape(64, 8, 1024)
        total = total + jnp.sum(parts, axis=0)
        square = square + jnp.sum(parts * parts, axis=0)
    total = jnp.sum(total, axis=0, keepdims=True)
    square = jnp.sum(square, axis=0, keepdims=True)
    total = sum(total[:, 128 * k : 128 * k + 128] for k in range(8))
    square = sum(square[:, 128 * k : 128 * k + 128] for k in range(8))
    for copy in copies:
        copy.wait()
    scale, offset = group_scale(total, square, 16384, 4, gain_ref[...], shift_ref[...])
    at = iota((192, 128), 0)
    first = (at & 31) == 0
    last = (at & 31) == 31
    start = pl.multiple_of(y * 128, 128)
    top = jnp.where(y > 0, 1.0, 0.0)
    bottom = jnp.where(y < 3, 1.0, 0.0)
    scale = scale * 0.5
    offset = offset * 0.5

    def act(val):
        half = val * scale + offset
        out = half + half * jnp.tanh(half)
        return jnp.concatenate([out[:32] * top, out[32:160], out[160:] * bottom], axis=0)

    def make_hidden(f):
        g, fo = divmod(f, 4)
        val = stem[g, pl.ds(start, 192), 256 * fo : 256 * fo + 256]
        even = act(val[:, :128])
        odd = act(val[:, 128:])
        before = jnp.where(first, 0.0, pltpu.roll(odd, 1, 0))
        after = jnp.where(last, 0.0, pltpu.roll(even, 191, 0))
        parts = (before - odd, even + odd, odd - even, even - after)
        for k, part in enumerate(parts):
            part = part.astype(BF16)
            hid[f + 2, :, 128 * k : 128 * k + 128] = part
            if f == 0:
                hid[0, :, 128 * k : 128 * k + 128] = part
                hid[1, :, 128 * k : 128 * k + 128] = part

    s = jnp.zeros((8, 256), F32)
    q = jnp.zeros((8, 256), F32)
    steps = [(a, b) for a in range(3) for b in range(3)]
    tail_even = jnp.concatenate([taps_ref[0, 1024:], taps_ref[1, 1024:]], axis=0)
    tail_odd = jnp.concatenate([taps_ref[1, 1024:], -taps_ref[3, 1024:]], axis=0)
    tail_both = taps_ref[2, 1024:]
    for k in range(16):
        make_hidden(k)
    for f in range(0, 16, 4):

        def tap(k, a, b):
            cut = hid[f + a : f + a + 4, 32 * b : 32 * b + 128, 128 * k : 128 * k + 128]
            return cut.reshape(512, 128)

        m = []
        for k in range(4):
            left = jnp.concatenate([tap(k, a, b) for a, b in steps[:8]], axis=1)
            m.append(jnp.dot(left, taps_ref[k, :1024], preferred_element_type=F32))
        t = [tap(k, 2, 2) for k in range(4)]
        even = jnp.dot(jnp.concatenate([t[0], t[1]], axis=1), tail_even, preferred_element_type=F32)
        odd = jnp.dot(jnp.concatenate([t[1], t[3]], axis=1), tail_odd, preferred_element_type=F32)
        both = jnp.dot(t[2], tail_both, preferred_element_type=F32) + m[2]
        even = even + m[0] + (m[1] + both)
        odd = odd - m[3] + (m[1] - both)
        for par, out in enumerate((even, odd)):
            mix_ref[par, f : f + 4] = out.reshape(4, 128, 256)
            parts = out.reshape(64, 8, 256)
            s = s + jnp.sum(parts, axis=0)
            q = q + jnp.sum(parts * parts, axis=0)
    stat_ref[0:1, :] = jnp.sum(s, axis=0, keepdims=True)
    stat_ref[1:2, :] = jnp.sum(q, axis=0, keepdims=True)


def quarter(to, mix_ref, scale, offset, dw_ref, bias_ref, out_ref, left):
    for g in range(2):
        for par in range(2):
            acts = []
            for i in range(2):
                half = mix_ref[par, 4 * to + 2 * g + i] * scale + offset
                acts.append(half + half * jnp.tanh(half))
            pooled = ((acts[0] + acts[1]) * 0.5).astype(BF16)
            for r in range(4):
                lane = ((r & 1) * 2 + par) * 256
                at = g * 64 + (r >> 1) * 32
                left[at : at + 32, lane : lane + 256] = pooled[32 * r : 32 * r + 32]
    out = jnp.dot(left[...], dw_ref[...], preferred_element_type=F32) + bias_ref[...]
    out_ref[...] = out.astype(BF16)


def first_kernel(
    by,
    me_ref,
    mix_ref,
    stat_a,
    stat_b,
    stat_c,
    stat_d,
    gain_ref,
    shift_ref,
    dw_ref,
    bias_ref,
    out_ref,
    affine_ref,
    left,
):
    stat = (stat_a[...] + stat_b[...]) + (stat_c[...] + stat_d[...])
    scale, offset = group_scale(
        stat[0:1, :], stat[1:2, :], 16384, 8, gain_ref[...], shift_ref[...]
    )
    scale = scale * 0.5
    offset = offset * 0.5
    affine_ref[0:1, :] = scale
    affine_ref[1:2, :] = offset
    quarter((me_ref[0] + by) & 3, mix_ref, scale, offset, dw_ref, bias_ref, out_ref, left)


def next_kernel(by, me_ref, mix_ref, affine_ref, dw_ref, bias_ref, out_ref, left):
    scale = affine_ref[0:1, :]
    offset = affine_ref[1:2, :]
    quarter((me_ref[0] + by) & 3, mix_ref, scale, offset, dw_ref, bias_ref, out_ref, left)


def place_kernel(me_ref, own, one, two, three, out_ref, sems):
    copies = [
        pltpu.make_async_copy(part, out_ref.at[(me_ref[0] + 4 - by) & 3], sems.at[by])
        for by, part in enumerate((own, one, two, three))
    ]
    for copy in copies:
        copy.start()
    for copy in copies:
        copy.wait()


def stem_places():
    place = np.zeros((8, 256, 81), np.float32)
    for fo in range(4):
        for par in range(2):
            for a in range(3):
                for b in range(3):
                    for c in range(3):
                        for ch in range(3):
                            row = b * 72 + (fo + a) * 12 + (par + c) * 3 + ch
                            place[fo * 2 + par, row, ((a * 3 + b) * 3 + c) * 3 + ch] = 1
    return place.reshape(2048, 81)


def in_hbm(array):
    return pltpu.with_memory_space_constraint(array, pltpu.HBM)


def call(kernel, out_shape, specs, scratch=(), mib=16):
    return pl.pallas_call(
        kernel,
        out_shape=out_shape,
        in_specs=specs,
        out_specs=jax.tree.map(lambda _: VMEM, out_shape),
        scratch_shapes=list(scratch),
        compiler_params=pltpu.CompilerParams(vmem_limit_bytes=mib << 20),
    )


def local(
    frames,
    keep_list,
    train_slot,
    stem_weight,
    stem_gain,
    stem_shift,
    mixer_weight,
    mixer_gain,
    mixer_shift,
    down_weight,
    down_bias,
):
    sds = jax.ShapeDtypeStruct
    index = lax.axis_index("clip")
    core = (index % 2).astype(jnp.int32).reshape(1)
    row = lax.axis_index("row").astype(jnp.int32).reshape(1)
    me = lax.axis_index("tm").astype(jnp.int32).reshape(1)
    core, row, me = lax.optimization_barrier((core, row, me))
    pairs = [(i, i ^ 1) for i in range(16)]
    frames_b = lax.ppermute(frames, "clip", pairs)
    keep_b = lax.ppermute(keep_list, "clip", pairs)
    keep_a, train, frames_a = call(
        fetch_kernel,
        (sds((8,), jnp.int32), sds((64,), jnp.int32), sds((8, 3, 4, 256), BF16)),
        [HBM] * 3,
        [pltpu.SemaphoreType.DMA((3,))],
    )(in_hbm(keep_list), in_hbm(train_slot), in_hbm(frames))
    packed = call(
        pack_kernel, sds((8, 4, 3, 4, 256), BF16), [SMEM] * 4 + [VMEM] * 2
    )(core, keep_a, keep_b, train, frames_a, frames_b)
    along_z = [[2 * z + k for z in range(8)] for k in range(2)]
    received = lax.all_to_all(
        packed, "clip", split_axis=0, concat_axis=0, tiled=True, axis_index_groups=along_z
    )
    pieces = call(
        combine_kernel, sds((16, 3, 4, 256), BF16), [VMEM], [pltpu.VMEM((48, 256), F32)]
    )(received)
    places = jnp.asarray(stem_places(), BF16)
    pieces, places = lax.optimization_barrier((pieces, places))
    w4, taps = call(
        weights_kernel,
        (sds((8, 256, 128), BF16), sds((4, 1152, 256), BF16)),
        [HBM] * 3,
        [
            pltpu.VMEM((2048, 81), BF16),
            pltpu.VMEM((81, 128), BF16),
            pltpu.VMEM((3456, 256), BF16),
            pltpu.SemaphoreType.DMA((3,)),
        ],
    )(in_hbm(places), in_hbm(stem_weight), in_hbm(mixer_weight.reshape(3456, 256)))
    raw = lax.all_to_all(pieces, ("row", "tm"), split_axis=0, concat_axis=0, tiled=True)
    mix, stat = call(
        mixer_kernel,
        (sds((2, 16, 128, 256), F32), sds((2, 256), F32)),
        [SMEM, VMEM, VMEM, HBM, HBM, VMEM],
        [
            pltpu.VMEM((2, 3, 16, 512), F32),
            pltpu.VMEM((3, 4, 216, 128), F32),
            pltpu.VMEM((4, 512, 256), BF16),
            pltpu.VMEM((4, 576, 1024), F32),
            pltpu.VMEM((18, 192, 512), BF16),
            pltpu.VMEM((1, 128), F32),
            pltpu.VMEM((1, 128), F32),
            pltpu.SemaphoreType.DMA((2,)),
        ],
        mib=24,
    )(
        row,
        raw,
        w4,
        in_hbm(stem_gain.reshape(1, -1)),
        in_hbm(stem_shift.reshape(1, -1)),
        taps,
    )
    others = [
        lax.ppermute(stat, "row", [(i, (i + by) % 4) for i in range(4)]) for by in (1, 2, 3)
    ]
    dw_bias = (down_weight, down_bias.reshape(1, -1))
    part = sds((128, 256), BF16)
    room = [pltpu.VMEM((128, 1024), BF16)]
    parts = {}

    def send(by):
        return lax.ppermute(parts[by], "tm", [(i, (i + by) % 4) for i in range(4)])

    parts[2], affine = call(
        functools.partial(first_kernel, 2),
        (part, sds((2, 256), F32)),
        [SMEM] + [VMEM] * 9,
        room,
    )(
        me,
        mix,
        stat,
        *others,
        mixer_gain.reshape(1, -1),
        mixer_shift.reshape(1, -1),
        *dw_bias,
    )
    parts[2] = send(2)
    for by in (1, 3, 0):
        parts[by] = call(
            functools.partial(next_kernel, by), part, [SMEM] + [VMEM] * 4, room
        )(me, mix, affine, *dw_bias)
        if by:
            parts[by] = send(by)
    placed = pl.pallas_call(
        place_kernel,
        out_shape=pltpu.HBM((4, 128, 256), BF16),
        in_specs=[SMEM] + [VMEM] * 4,
        out_specs=HBM,
        scratch_shapes=[pltpu.SemaphoreType.DMA((4,))],
        compiler_params=pltpu.CompilerParams(vmem_limit_bytes=1 << 20),
    )(me, *(parts[by] for by in range(4)))
    return placed.reshape(4, 2, 2, 32, 256)


def solution(mesh):
    return jax.shard_map(
        local,
        mesh=mesh,
        in_specs=(P("clip", None, "tm", "row"), P("clip")) + (P(),) * 9,
        out_specs=P("clip", "tm", "row", None, None),
        check_vma=False,
    )
```

```python
import functools

import jax
import jax.numpy as jnp
import numpy as np
from jax import lax
from jax.experimental import pallas as pl
from jax.experimental.pallas import tpu as pltpu
from jax.sharding import PartitionSpec as P

F32 = jnp.float32
BF16 = jnp.bfloat16
eps = 1e-06

VMEM = pl.BlockSpec(memory_space=pltpu.VMEM)
SMEM = pl.BlockSpec(memory_space=pltpu.SMEM)
ANY = pl.BlockSpec(memory_space=pl.ANY)
HBM = pl.BlockSpec(memory_space=pltpu.HBM)


def iota(shape, dim):
    return lax.broadcasted_iota(jnp.int32, shape, dim)


def weights_kernel(places_hbm, stem_hbm, mw_hbm, w4_ref, taps_ref, places, stem, mw, sems):
    pairs = ((places_hbm, places), (stem_hbm, stem), (mw_hbm, mw))
    copies = [pltpu.make_async_copy(src, dst, sems.at[i]) for i, (src, dst) in enumerate(pairs)]
    for copy in copies:
        copy.start()
    copies[0].wait()
    copies[1].wait()
    for n in range(8):
        part = places[256 * n : 256 * n + 256, :]
        w4_ref[n] = jnp.dot(part, stem[...], preferred_element_type=F32).astype(BF16)
    copies[2].wait()
    for k in range(9):
        g0, g1, g2 = (mw[384 * k + 128 * c : 384 * k + 128 * c + 128] for c in range(3))
        outer = (g0.astype(F32) + g2.astype(F32)) * 0.5
        inner = g1.astype(F32) * 0.5
        at = slice(128 * k, 128 * k + 128)
        taps_ref[0, at] = g0
        taps_ref[1, at] = (outer + inner).astype(BF16)
        taps_ref[2, at] = (outer - inner).astype(BF16)
        taps_ref[3, at] = g2


def fetch_kernel(keep, train, fr, keep_out, train_out, fr_out, sems):
    pairs = ((keep, keep_out), (train, train_out), (fr, fr_out))
    copies = [pltpu.make_async_copy(src, dst, sems.at[i]) for i, (src, dst) in enumerate(pairs)]
    for copy in copies:
        copy.start()
    for copy in copies:
        copy.wait()


def pack_kernel(core_ref, keep_s, keep_t, train_s, fra, frb, out_ref):
    out_ref[...] = jnp.zeros_like(out_ref)
    core = core_ref[0]
    for keep_ref, fr in ((keep_s, fra), (keep_t, frb)):
        for j in range(fr.shape[0]):
            k = keep_ref[j]
            t = train_s[jnp.maximum(k, 0)]
            mine = jnp.logical_and(k >= 0, ((t >> 2) & 1) == core)

            @pl.when(mine)
            def _():
                out_ref[t >> 3, t & 3] = fr[j]


def combine_kernel(recv_ref, out_ref, rows_ref):
    for k in range(4):
        for ch in range(3):
            total = recv_ref[0, k, ch].astype(F32)
            for s in range(1, recv_ref.shape[0]):
                total = total + recv_ref[s, k, ch].astype(F32)
            at = (k * 3 + ch) * 4
            rows_ref[at : at + 4, :] = total
    i = iota((256, 256), 0)
    o = iota((256, 256), 1)
    source = ((o >> 5) & 3) * 64 + (o & 31) * 2 + (o >> 7)
    pick = (i == source).astype(F32).astype(BF16)
    split = jnp.dot(rows_ref[...].astype(BF16), pick, preferred_element_type=F32)
    rows_ref[...] = split
    for k in range(4):
        for ch in range(3):
            at = (k * 3 + ch) * 4
            piece = rows_ref[at : at + 4, :].astype(BF16)
            for y in range(4):
                out_ref[y * 4 + k, ch] = piece


def group_scale(total, square, cells, per_group, gain, shift):
    n = total.shape[1]
    gi = iota((n, n), 0) // per_group
    gj = iota((n, n), 1) // per_group
    member = (gi == gj).astype(F32).astype(BF16)
    both = jnp.concatenate([total, square, jnp.zeros((6, n), F32)], axis=0)
    high = both.astype(BF16).astype(F32)
    rest = both - high
    middle = rest.astype(BF16).astype(F32)
    split = jnp.concatenate([high, middle, rest - middle, jnp.zeros((8, n), F32)], axis=0)
    sums = jnp.dot(split.astype(BF16), member, preferred_element_type=F32)
    sums = sums[0:8] + (sums[8:16] + sums[16:24])
    sums = sums * (1.0 / (cells * per_group))
    mean = sums[0:1]
    spread = sums[1:2] - mean * mean
    scale = gain * lax.rsqrt(spread + eps)
    return scale, shift - mean * scale


def mixer_kernel(
    y_ref,
    raw_ref,
    w4_ref,
    gain_hbm,
    shift_hbm,
    taps_ref,
    mix_ref,
    stat_ref,
    dv,
    rows,
    tg,
    stem,
    hid,
    gain_ref,
    shift_ref,
    sems,
):
    y = y_ref[0]
    copies = [
        pltpu.make_async_copy(gain_hbm, gain_ref, sems.at[0]),
        pltpu.make_async_copy(shift_hbm, shift_ref, sems.at[1]),
    ]
    for copy in copies:
        copy.start()
    for yy in range(4):
        for xx in range(4):
            for ch in range(3):
                piece = raw_ref[yy * 4 + xx, ch].astype(F32)
                for par in range(2):
                    dv[par, ch, 4 * xx : 4 * xx + 4, 128 * yy : 128 * yy + 128] = piece[
                        :, 128 * par : 128 * par + 128
                    ]
    lane = iota((16, 512), 1)
    pair = lane & 31
    for ch in range(3):
        even = dv[0, ch]
        odd = dv[1, ch]
        before = jnp.where(pair == 0, 0.0, pltpu.roll(odd, 1, 1))
        after = jnp.where(pair == 31, 0.0, pltpu.roll(even, 511, 1))
        for v, plane in enumerate((before, even, odd, after)):
            above = jnp.where(lane < 32, 0.0, pltpu.roll(plane, 32, 1))
            below = jnp.where(lane >= 480, 0.0, pltpu.roll(plane, 480, 1))
            at = v * 3 + ch
            for b, part in enumerate((above, plane, below)):
                for j in range(4):
                    cut = part[:, 128 * j : 128 * j + 128]
                    rows[b, j, pl.ds(24 + at, 16, stride=12), :] = cut
                    rows[b, j, at : at + 1, :] = cut[0:1]
                    rows[b, j, 12 + at : 13 + at, :] = cut[0:1]
    for g in range(4):
        for j in range(4):
            taps = [rows[b, j, 48 * g : 48 * g + 72, :] for b in range(3)]
            block = jnp.concatenate(taps + [jnp.zeros((40, 128), F32)], axis=0)
            tg[g, 128 * j : 128 * j + 128, :] = jnp.transpose(block).astype(BF16)
    total = jnp.zeros((8, 1024), F32)
    square = jnp.zeros((8, 1024), F32)
    for g in range(4):
        stem[g, 0:32, :] = jnp.zeros((32, 1024), F32)
        stem[g, 544:576, :] = jnp.zeros((32, 1024), F32)
        w4 = jnp.concatenate([w4_ref[n] for n in range(8)], axis=1)
        out = jnp.dot(tg[g], w4, preferred_element_type=F32)
        stem[g, 32:544, :] = out
        parts = out.reshape(64, 8, 1024)
        total = total + jnp.sum(parts, axis=0)
        square = square + jnp.sum(parts * parts, axis=0)
    total = jnp.sum(total, axis=0, keepdims=True)
    square = jnp.sum(square, axis=0, keepdims=True)
    total = sum(total[:, 128 * k : 128 * k + 128] for k in range(8))
    square = sum(square[:, 128 * k : 128 * k + 128] for k in range(8))
    for copy in copies:
        copy.wait()
    scale, offset = group_scale(total, square, 16384, 4, gain_ref[...], shift_ref[...])
    at = iota((192, 128), 0)
    first = (at & 31) == 0
    last = (at & 31) == 31
    start = pl.multiple_of(y * 128, 128)
    top = jnp.where(y > 0, 1.0, 0.0)
    bottom = jnp.where(y < 3, 1.0, 0.0)
    scale = scale * 0.5
    offset = offset * 0.5

    def act(val):
        half = val * scale + offset
        out = half + half * jnp.tanh(half)
        return jnp.concatenate([out[:32] * top, out[32:160], out[160:] * bottom], axis=0)

    def make_hidden(f):
        g, fo = divmod(f, 4)
        val = stem[g, pl.ds(start, 192), 256 * fo : 256 * fo + 256]
        even = act(val[:, :128])
        odd = act(val[:, 128:])
        before = jnp.where(first, 0.0, pltpu.roll(odd, 1, 0))
        after = jnp.where(last, 0.0, pltpu.roll(even, 191, 0))
        parts = (before - odd, even + odd, odd - even, even - after)
        for k, part in enumerate(parts):
            part = part.astype(BF16)
            hid[f + 2, :, 128 * k : 128 * k + 128] = part
            if f == 0:
                hid[0, :, 128 * k : 128 * k + 128] = part
                hid[1, :, 128 * k : 128 * k + 128] = part

    s = jnp.zeros((8, 256), F32)
    q = jnp.zeros((8, 256), F32)
    steps = [(a, b) for a in range(3) for b in range(3)]
    tail_even = jnp.concatenate([taps_ref[0, 1024:], taps_ref[1, 1024:]], axis=0)
    tail_odd = jnp.concatenate([taps_ref[1, 1024:], -taps_ref[3, 1024:]], axis=0)
    tail_both = taps_ref[2, 1024:]
    for k in range(16):
        make_hidden(k)
    for f in range(0, 16, 4):

        def tap(k, a, b):
            cut = hid[f + a : f + a + 4, 32 * b : 32 * b + 128, 128 * k : 128 * k + 128]
            return cut.reshape(512, 128)

        m = []
        for k in range(4):
            left = jnp.concatenate([tap(k, a, b) for a, b in steps[:8]], axis=1)
            m.append(jnp.dot(left, taps_ref[k, :1024], preferred_element_type=F32))
        t = [tap(k, 2, 2) for k in range(4)]
        even = jnp.dot(jnp.concatenate([t[0], t[1]], axis=1), tail_even, preferred_element_type=F32)
        odd = jnp.dot(jnp.concatenate([t[1], t[3]], axis=1), tail_odd, preferred_element_type=F32)
        both = jnp.dot(t[2], tail_both, preferred_element_type=F32) + m[2]
        even = even + m[0] + (m[1] + both)
        odd = odd - m[3] + (m[1] - both)
        for par, out in enumerate((even, odd)):
            mix_ref[par, f : f + 4] = out.reshape(4, 128, 256)
            parts = out.reshape(64, 8, 256)
            s = s + jnp.sum(parts, axis=0)
            q = q + jnp.sum(parts * parts, axis=0)
    stat_ref[0:1, :] = jnp.sum(s, axis=0, keepdims=True)
    stat_ref[1:2, :] = jnp.sum(q, axis=0, keepdims=True)


def quarter(to, mix_ref, scale, offset, dw_ref, bias_ref, out_ref, left):
    for g in range(2):
        for par in range(2):
            acts = []
            for i in range(2):
                half = mix_ref[par, 4 * to + 2 * g + i] * scale + offset
                acts.append(half + half * jnp.tanh(half))
            pooled = ((acts[0] + acts[1]) * 0.5).astype(BF16)
            for r in range(4):
                lane = ((r & 1) * 2 + par) * 256
                at = g * 64 + (r >> 1) * 32
                left[at : at + 32, lane : lane + 256] = pooled[32 * r : 32 * r + 32]
    out = jnp.dot(left[...], dw_ref[...], preferred_element_type=F32) + bias_ref[...]
    out_ref[...] = out.astype(BF16)


def first_kernel(
    by,
    me_ref,
    mix_ref,
    stat_a,
    stat_b,
    stat_c,
    stat_d,
    gain_ref,
    shift_ref,
    dw_ref,
    bias_ref,
    out_ref,
    affine_ref,
    left,
):
    stat = (stat_a[...] + stat_b[...]) + (stat_c[...] + stat_d[...])
    scale, offset = group_scale(
        stat[0:1, :], stat[1:2, :], 16384, 8, gain_ref[...], shift_ref[...]
    )
    scale = scale * 0.5
    offset = offset * 0.5
    affine_ref[0:1, :] = scale
    affine_ref[1:2, :] = offset
    quarter((me_ref[0] + by) & 3, mix_ref, scale, offset, dw_ref, bias_ref, out_ref, left)


def next_kernel(by, me_ref, mix_ref, affine_ref, dw_ref, bias_ref, out_ref, left):
    scale = affine_ref[0:1, :]
    offset = affine_ref[1:2, :]
    quarter((me_ref[0] + by) & 3, mix_ref, scale, offset, dw_ref, bias_ref, out_ref, left)


def place_kernel(me_ref, own, one, two, three, out_ref, sems):
    copies = [
        pltpu.make_async_copy(part, out_ref.at[(me_ref[0] + 4 - by) & 3], sems.at[by])
        for by, part in enumerate((own, one, two, three))
    ]
    for copy in copies:
        copy.start()
    for copy in copies:
        copy.wait()


def stem_places():
    place = np.zeros((8, 256, 81), np.float32)
    for fo in range(4):
        for par in range(2):
            for a in range(3):
                for b in range(3):
                    for c in range(3):
                        for ch in range(3):
                            row = b * 72 + (fo + a) * 12 + (par + c) * 3 + ch
                            place[fo * 2 + par, row, ((a * 3 + b) * 3 + c) * 3 + ch] = 1
    return place.reshape(2048, 81)


def in_hbm(array):
    return pltpu.with_memory_space_constraint(array, pltpu.HBM)


def call(kernel, out_shape, specs, scratch=(), mib=16):
    return pl.pallas_call(
        kernel,
        out_shape=out_shape,
        in_specs=specs,
        out_specs=jax.tree.map(lambda _: VMEM, out_shape),
        scratch_shapes=list(scratch),
        compiler_params=pltpu.CompilerParams(vmem_limit_bytes=mib << 20),
    )


def local(
    frames,
    keep_list,
    train_slot,
    stem_weight,
    stem_gain,
    stem_shift,
    mixer_weight,
    mixer_gain,
    mixer_shift,
    down_weight,
    down_bias,
):
    sds = jax.ShapeDtypeStruct
    index = lax.axis_index("clip")
    core = (index % 2).astype(jnp.int32).reshape(1)
    row = lax.axis_index("row").astype(jnp.int32).reshape(1)
    me = lax.axis_index("tm").astype(jnp.int32).reshape(1)
    core, row, me = lax.optimization_barrier((core, row, me))
    pairs = [(i, i ^ 1) for i in range(16)]
    frames_b = lax.ppermute(frames, "clip", pairs)
    keep_b = lax.ppermute(keep_list, "clip", pairs)
    keep_a, train, frames_a = call(
        fetch_kernel,
        (sds((8,), jnp.int32), sds((64,), jnp.int32), sds((8, 3, 4, 256), BF16)),
        [HBM] * 3,
        [pltpu.SemaphoreType.DMA((3,))],
    )(in_hbm(keep_list), in_hbm(train_slot), in_hbm(frames))
    packed = call(
        pack_kernel, sds((8, 4, 3, 4, 256), BF16), [SMEM] * 4 + [VMEM] * 2
    )(core, keep_a, keep_b, train, frames_a, frames_b)
    along_z = [[2 * z + k for z in range(8)] for k in range(2)]
    received = lax.all_to_all(
        packed, "clip", split_axis=0, concat_axis=0, tiled=True, axis_index_groups=along_z
    )
    pieces = call(
        combine_kernel, sds((16, 3, 4, 256), BF16), [VMEM], [pltpu.VMEM((48, 256), F32)]
    )(received)
    places = jnp.asarray(stem_places(), BF16)
    pieces, places = lax.optimization_barrier((pieces, places))
    w4, taps = call(
        weights_kernel,
        (sds((8, 256, 128), BF16), sds((4, 1152, 256), BF16)),
        [HBM] * 3,
        [
            pltpu.VMEM((2048, 81), BF16),
            pltpu.VMEM((81, 128), BF16),
            pltpu.VMEM((3456, 256), BF16),
            pltpu.SemaphoreType.DMA((3,)),
        ],
    )(in_hbm(places), in_hbm(stem_weight), in_hbm(mixer_weight.reshape(3456, 256)))
    raw = lax.all_to_all(pieces, ("row", "tm"), split_axis=0, concat_axis=0, tiled=True)
    mix, stat = call(
        mixer_kernel,
        (sds((2, 16, 128, 256), F32), sds((2, 256), F32)),
        [SMEM, VMEM, VMEM, HBM, HBM, VMEM],
        [
            pltpu.VMEM((2, 3, 16, 512), F32),
            pltpu.VMEM((3, 4, 216, 128), F32),
            pltpu.VMEM((4, 512, 256), BF16),
            pltpu.VMEM((4, 576, 1024), F32),
            pltpu.VMEM((18, 192, 512), BF16),
            pltpu.VMEM((1, 128), F32),
            pltpu.VMEM((1, 128), F32),
            pltpu.SemaphoreType.DMA((2,)),
        ],
        mib=24,
    )(
        row,
        raw,
        w4,
        in_hbm(stem_gain.reshape(1, -1)),
        in_hbm(stem_shift.reshape(1, -1)),
        taps,
    )
    others = [
        lax.ppermute(stat, "row", [(i, (i + by) % 4) for i in range(4)]) for by in (1, 2, 3)
    ]
    dw_bias = (down_weight, down_bias.reshape(1, -1))
    part = sds((128, 256), BF16)
    room = [pltpu.VMEM((128, 1024), BF16)]
    parts = {}

    def send(by):
        return lax.ppermute(parts[by], "tm", [(i, (i + by) % 4) for i in range(4)])

    parts[3], affine = call(
        functools.partial(first_kernel, 3),
        (part, sds((2, 256), F32)),
        [SMEM] + [VMEM] * 9,
        room,
    )(
        me,
        mix,
        stat,
        *others,
        mixer_gain.reshape(1, -1),
        mixer_shift.reshape(1, -1),
        *dw_bias,
    )
    parts[3] = send(3)
    for by in (2, 1, 0):
        parts[by] = call(
            functools.partial(next_kernel, by), part, [SMEM] + [VMEM] * 4, room
        )(me, mix, affine, *dw_bias)
        if by:
            parts[by] = send(by)
    placed = pl.pallas_call(
        place_kernel,
        out_shape=pltpu.HBM((4, 128, 256), BF16),
        in_specs=[SMEM] + [VMEM] * 4,
        out_specs=HBM,
        scratch_shapes=[pltpu.SemaphoreType.DMA((4,))],
        compiler_params=pltpu.CompilerParams(vmem_limit_bytes=1 << 20),
    )(me, *(parts[by] for by in range(4)))
    return placed.reshape(4, 2, 2, 32, 256)


def solution(mesh):
    return jax.shard_map(
        local,
        mesh=mesh,
        in_specs=(P("clip", None, "tm", "row"), P("clip")) + (P(),) * 9,
        out_specs=P("clip", "tm", "row", None, None),
        check_vma=False,
    )
```

```python
import functools

import jax
import jax.numpy as jnp
import numpy as np
from jax import lax
from jax.experimental import pallas as pl
from jax.experimental.pallas import tpu as pltpu
from jax.sharding import PartitionSpec as P

F32 = jnp.float32
BF16 = jnp.bfloat16
eps = 1e-06

VMEM = pl.BlockSpec(memory_space=pltpu.VMEM)
SMEM = pl.BlockSpec(memory_space=pltpu.SMEM)
ANY = pl.BlockSpec(memory_space=pl.ANY)
HBM = pl.BlockSpec(memory_space=pltpu.HBM)


def iota(shape, dim):
    return lax.broadcasted_iota(jnp.int32, shape, dim)


def weights_kernel(
    places_hbm, stem_hbm, mw_hbm, w4_ref, taps_ref, places, stem, mw, padded, sems
):
    pairs = ((places_hbm, places), (stem_hbm, stem), (mw_hbm, mw))
    copies = [pltpu.make_async_copy(src, dst, sems.at[i]) for i, (src, dst) in enumerate(pairs)]
    for copy in copies:
        copy.start()
    padded[...] = jnp.zeros_like(padded)
    copies[0].wait()
    copies[1].wait()
    padded[0:81, :] = stem[...]
    for n in range(8):
        part = places[256 * n : 256 * n + 256, :]
        w4_ref[n] = jnp.dot(part, padded[...], preferred_element_type=F32).astype(BF16)
    copies[2].wait()
    for k in range(9):
        g0, g1, g2 = (mw[384 * k + 128 * c : 384 * k + 128 * c + 128] for c in range(3))
        outer = (g0.astype(F32) + g2.astype(F32)) * 0.5
        inner = g1.astype(F32) * 0.5
        at = slice(128 * k, 128 * k + 128)
        taps_ref[0, at] = g0
        taps_ref[1, at] = (outer + inner).astype(BF16)
        taps_ref[2, at] = (outer - inner).astype(BF16)
        taps_ref[3, at] = g2


def fetch_kernel(keep, train, fr, keep_out, train_out, fr_out, sems):
    pairs = ((keep, keep_out), (train, train_out), (fr, fr_out))
    copies = [pltpu.make_async_copy(src, dst, sems.at[i]) for i, (src, dst) in enumerate(pairs)]
    for copy in copies:
        copy.start()
    for copy in copies:
        copy.wait()


def pack_kernel(core_ref, keep_s, keep_t, train_s, fra, frb, out_ref):
    out_ref[...] = jnp.zeros_like(out_ref)
    core = core_ref[0]
    for keep_ref, fr in ((keep_s, fra), (keep_t, frb)):
        for j in range(fr.shape[0]):
            k = keep_ref[j]
            t = train_s[jnp.maximum(k, 0)]
            mine = jnp.logical_and(k >= 0, ((t >> 2) & 1) == core)

            @pl.when(mine)
            def _():
                out_ref[t >> 3, t & 3] = fr[j]


def combine_kernel(recv_ref, out_ref, rows_ref):
    for k in range(4):
        for ch in range(3):
            total = recv_ref[0, k, ch].astype(F32)
            for s in range(1, recv_ref.shape[0]):
                total = total + recv_ref[s, k, ch].astype(F32)
            at = (k * 3 + ch) * 4
            rows_ref[at : at + 4, :] = total
    i = iota((256, 256), 0)
    o = iota((256, 256), 1)
    source = ((o >> 5) & 3) * 64 + (o & 31) * 2 + (o >> 7)
    pick = (i == source).astype(F32).astype(BF16)
    split = jnp.dot(rows_ref[...].astype(BF16), pick, preferred_element_type=F32)
    rows_ref[...] = split
    for k in range(4):
        for ch in range(3):
            at = (k * 3 + ch) * 4
            piece = rows_ref[at : at + 4, :].astype(BF16)
            for y in range(4):
                out_ref[y * 4 + k, ch] = piece


def group_scale(total, square, cells, per_group, gain, shift):
    n = total.shape[1]
    gi = iota((n, n), 0) // per_group
    gj = iota((n, n), 1) // per_group
    member = (gi == gj).astype(F32).astype(BF16)
    both = jnp.concatenate([total, square, jnp.zeros((6, n), F32)], axis=0)
    high = both.astype(BF16).astype(F32)
    rest = both - high
    middle = rest.astype(BF16).astype(F32)
    split = jnp.concatenate([high, middle, rest - middle, jnp.zeros((8, n), F32)], axis=0)
    sums = jnp.dot(split.astype(BF16), member, preferred_element_type=F32)
    sums = sums[0:8] + (sums[8:16] + sums[16:24])
    sums = sums * (1.0 / (cells * per_group))
    mean = sums[0:1]
    spread = sums[1:2] - mean * mean
    scale = gain * lax.rsqrt(spread + eps)
    return scale, shift - mean * scale


def mixer_kernel(
    y_ref,
    raw_ref,
    w4_ref,
    gain_hbm,
    shift_hbm,
    taps_ref,
    mix_ref,
    stat_ref,
    dv,
    rows,
    tg,
    stem,
    hid,
    gain_ref,
    shift_ref,
    sems,
):
    y = y_ref[0]
    copies = [
        pltpu.make_async_copy(gain_hbm, gain_ref, sems.at[0]),
        pltpu.make_async_copy(shift_hbm, shift_ref, sems.at[1]),
    ]
    for copy in copies:
        copy.start()
    for yy in range(4):
        for xx in range(4):
            for ch in range(3):
                piece = raw_ref[yy * 4 + xx, ch].astype(F32)
                for par in range(2):
                    dv[par, ch, 4 * xx : 4 * xx + 4, 128 * yy : 128 * yy + 128] = piece[
                        :, 128 * par : 128 * par + 128
                    ]
    lane = iota((16, 512), 1)
    pair = lane & 31
    for ch in range(3):
        even = dv[0, ch]
        odd = dv[1, ch]
        before = jnp.where(pair == 0, 0.0, pltpu.roll(odd, 1, 1))
        after = jnp.where(pair == 31, 0.0, pltpu.roll(even, 511, 1))
        for v, plane in enumerate((before, even, odd, after)):
            above = jnp.where(lane < 32, 0.0, pltpu.roll(plane, 32, 1))
            below = jnp.where(lane >= 480, 0.0, pltpu.roll(plane, 480, 1))
            at = v * 3 + ch
            for b, part in enumerate((above, plane, below)):
                for j in range(4):
                    cut = part[:, 128 * j : 128 * j + 128]
                    rows[b, j, pl.ds(24 + at, 16, stride=12), :] = cut
                    rows[b, j, at : at + 1, :] = cut[0:1]
                    rows[b, j, 12 + at : 13 + at, :] = cut[0:1]
    for g in range(4):
        for j in range(4):
            taps = [rows[b, j, 48 * g : 48 * g + 72, :] for b in range(3)]
            block = jnp.concatenate(taps + [jnp.zeros((40, 128), F32)], axis=0)
            tg[g, 128 * j : 128 * j + 128, :] = jnp.transpose(block).astype(BF16)
    total = jnp.zeros((8, 1024), F32)
    square = jnp.zeros((8, 1024), F32)
    for g in range(4):
        stem[g, 0:32, :] = jnp.zeros((32, 1024), F32)
        stem[g, 544:576, :] = jnp.zeros((32, 1024), F32)
        w4 = jnp.concatenate([w4_ref[n] for n in range(8)], axis=1)
        out = jnp.dot(tg[g], w4, preferred_element_type=F32)
        stem[g, 32:544, :] = out
        parts = out.reshape(64, 8, 1024)
        total = total + jnp.sum(parts, axis=0)
        square = square + jnp.sum(parts * parts, axis=0)
    total = jnp.sum(total, axis=0, keepdims=True)
    square = jnp.sum(square, axis=0, keepdims=True)
    total = sum(total[:, 128 * k : 128 * k + 128] for k in range(8))
    square = sum(square[:, 128 * k : 128 * k + 128] for k in range(8))
    for copy in copies:
        copy.wait()
    scale, offset = group_scale(total, square, 16384, 4, gain_ref[...], shift_ref[...])
    at = iota((192, 128), 0)
    first = (at & 31) == 0
    last = (at & 31) == 31
    start = pl.multiple_of(y * 128, 128)
    top = jnp.where(y > 0, 1.0, 0.0)
    bottom = jnp.where(y < 3, 1.0, 0.0)
    scale = scale * 0.5
    offset = offset * 0.5

    def act(val):
        half = val * scale + offset
        out = half + half * jnp.tanh(half)
        return jnp.concatenate([out[:32] * top, out[32:160], out[160:] * bottom], axis=0)

    def make_hidden(f):
        g, fo = divmod(f, 4)
        val = stem[g, pl.ds(start, 192), 256 * fo : 256 * fo + 256]
        even = act(val[:, :128])
        odd = act(val[:, 128:])
        before = jnp.where(first, 0.0, pltpu.roll(odd, 1, 0))
        after = jnp.where(last, 0.0, pltpu.roll(even, 191, 0))
        parts = (before - odd, even + odd, odd - even, even - after)
        for k, part in enumerate(parts):
            part = part.astype(BF16)
            hid[f + 2, :, 128 * k : 128 * k + 128] = part
            if f == 0:
                hid[0, :, 128 * k : 128 * k + 128] = part
                hid[1, :, 128 * k : 128 * k + 128] = part

    s = jnp.zeros((8, 256), F32)
    q = jnp.zeros((8, 256), F32)
    steps = [(a, b) for a in range(3) for b in range(3)]
    tail_even = jnp.concatenate([taps_ref[0, 1024:], taps_ref[1, 1024:]], axis=0)
    tail_odd = jnp.concatenate([taps_ref[1, 1024:], -taps_ref[3, 1024:]], axis=0)
    tail_both = jnp.concatenate([taps_ref[2, 1024:], jnp.zeros((128, 256), BF16)], axis=0)
    blank = jnp.zeros((512, 128), BF16)
    for k in range(16):
        make_hidden(k)
    for f in range(0, 16, 4):

        def tap(k, a, b):
            cut = hid[f + a : f + a + 4, 32 * b : 32 * b + 128, 128 * k : 128 * k + 128]
            return cut.reshape(512, 128)

        m = []
        for k in range(4):
            left = jnp.concatenate([tap(k, a, b) for a, b in steps[:8]], axis=1)
            m.append(jnp.dot(left, taps_ref[k, :1024], preferred_element_type=F32))
        t = [tap(k, 2, 2) for k in range(4)]
        even = jnp.dot(jnp.concatenate([t[0], t[1]], axis=1), tail_even, preferred_element_type=F32)
        odd = jnp.dot(jnp.concatenate([t[1], t[3]], axis=1), tail_odd, preferred_element_type=F32)
        both = jnp.concatenate([t[2], blank], axis=1)
        both = jnp.dot(both, tail_both, preferred_element_type=F32) + m[2]
        even = even + m[0] + (m[1] + both)
        odd = odd - m[3] + (m[1] - both)
        for par, out in enumerate((even, odd)):
            mix_ref[par, f : f + 4] = out.reshape(4, 128, 256)
            parts = out.reshape(64, 8, 256)
            s = s + jnp.sum(parts, axis=0)
            q = q + jnp.sum(parts * parts, axis=0)
    stat_ref[0:1, :] = jnp.sum(s, axis=0, keepdims=True)
    stat_ref[1:2, :] = jnp.sum(q, axis=0, keepdims=True)


def quarter(to, mix_ref, scale, offset, dw_ref, bias_ref, out_ref, left):
    for g in range(2):
        for par in range(2):
            acts = []
            for i in range(2):
                half = mix_ref[par, 4 * to + 2 * g + i] * scale + offset
                acts.append(half + half * jnp.tanh(half))
            pooled = ((acts[0] + acts[1]) * 0.5).astype(BF16)
            for r in range(4):
                lane = ((r & 1) * 2 + par) * 256
                at = g * 64 + (r >> 1) * 32
                left[at : at + 32, lane : lane + 256] = pooled[32 * r : 32 * r + 32]
    out = jnp.dot(left[...], dw_ref[...], preferred_element_type=F32) + bias_ref[...]
    out_ref[...] = out.astype(BF16)


def first_kernel(
    by,
    me_ref,
    mix_ref,
    stat_a,
    stat_b,
    stat_c,
    stat_d,
    gain_ref,
    shift_ref,
    dw_ref,
    bias_ref,
    out_ref,
    affine_ref,
    left,
):
    stat = (stat_a[...] + stat_b[...]) + (stat_c[...] + stat_d[...])
    scale, offset = group_scale(
        stat[0:1, :], stat[1:2, :], 16384, 8, gain_ref[...], shift_ref[...]
    )
    scale = scale * 0.5
    offset = offset * 0.5
    affine_ref[0:1, :] = scale
    affine_ref[1:2, :] = offset
    quarter((me_ref[0] + by) & 3, mix_ref, scale, offset, dw_ref, bias_ref, out_ref, left)


def next_kernel(by, me_ref, mix_ref, affine_ref, dw_ref, bias_ref, out_ref, left):
    scale = affine_ref[0:1, :]
    offset = affine_ref[1:2, :]
    quarter((me_ref[0] + by) & 3, mix_ref, scale, offset, dw_ref, bias_ref, out_ref, left)


def place_kernel(me_ref, own, one, two, three, out_ref, sems):
    copies = [
        pltpu.make_async_copy(part, out_ref.at[(me_ref[0] + 4 - by) & 3], sems.at[by])
        for by, part in enumerate((own, one, two, three))
    ]
    for copy in copies:
        copy.start()
    for copy in copies:
        copy.wait()


def stem_places():
    place = np.zeros((8, 256, 128), np.float32)
    for fo in range(4):
        for par in range(2):
            for a in range(3):
                for b in range(3):
                    for c in range(3):
                        for ch in range(3):
                            row = b * 72 + (fo + a) * 12 + (par + c) * 3 + ch
                            place[fo * 2 + par, row, ((a * 3 + b) * 3 + c) * 3 + ch] = 1
    return place.reshape(2048, 128)


def in_hbm(array):
    return pltpu.with_memory_space_constraint(array, pltpu.HBM)


def call(kernel, out_shape, specs, scratch=(), mib=16):
    return pl.pallas_call(
        kernel,
        out_shape=out_shape,
        in_specs=specs,
        out_specs=jax.tree.map(lambda _: VMEM, out_shape),
        scratch_shapes=list(scratch),
        compiler_params=pltpu.CompilerParams(vmem_limit_bytes=mib << 20),
    )


def local(
    frames,
    keep_list,
    train_slot,
    stem_weight,
    stem_gain,
    stem_shift,
    mixer_weight,
    mixer_gain,
    mixer_shift,
    down_weight,
    down_bias,
):
    sds = jax.ShapeDtypeStruct
    index = lax.axis_index("clip")
    core = (index % 2).astype(jnp.int32).reshape(1)
    row = lax.axis_index("row").astype(jnp.int32).reshape(1)
    me = lax.axis_index("tm").astype(jnp.int32).reshape(1)
    core, row, me = lax.optimization_barrier((core, row, me))
    pairs = [(i, i ^ 1) for i in range(16)]
    frames_b = lax.ppermute(frames, "clip", pairs)
    keep_b = lax.ppermute(keep_list, "clip", pairs)
    keep_a, train, frames_a = call(
        fetch_kernel,
        (sds((8,), jnp.int32), sds((64,), jnp.int32), sds((8, 3, 4, 256), BF16)),
        [HBM] * 3,
        [pltpu.SemaphoreType.DMA((3,))],
    )(in_hbm(keep_list), in_hbm(train_slot), in_hbm(frames))
    packed = call(
        pack_kernel, sds((8, 4, 3, 4, 256), BF16), [SMEM] * 4 + [VMEM] * 2
    )(core, keep_a, keep_b, train, frames_a, frames_b)
    along_z = [[2 * z + k for z in range(8)] for k in range(2)]
    received = lax.all_to_all(
        packed, "clip", split_axis=0, concat_axis=0, tiled=True, axis_index_groups=along_z
    )
    pieces = call(
        combine_kernel, sds((16, 3, 4, 256), BF16), [VMEM], [pltpu.VMEM((48, 256), F32)]
    )(received)
    places = jnp.asarray(stem_places(), BF16)
    pieces, places = lax.optimization_barrier((pieces, places))
    w4, taps = call(
        weights_kernel,
        (sds((8, 256, 128), BF16), sds((4, 1152, 256), BF16)),
        [HBM] * 3,
        [
            pltpu.VMEM((2048, 128), BF16),
            pltpu.VMEM((81, 128), BF16),
            pltpu.VMEM((3456, 256), BF16),
            pltpu.VMEM((128, 128), BF16),
            pltpu.SemaphoreType.DMA((3,)),
        ],
    )(in_hbm(places), in_hbm(stem_weight), in_hbm(mixer_weight.reshape(3456, 256)))
    raw = lax.all_to_all(pieces, ("row", "tm"), split_axis=0, concat_axis=0, tiled=True)
    mix, stat = call(
        mixer_kernel,
        (sds((2, 16, 128, 256), F32), sds((2, 256), F32)),
        [SMEM, VMEM, VMEM, HBM, HBM, VMEM],
        [
            pltpu.VMEM((2, 3, 16, 512), F32),
            pltpu.VMEM((3, 4, 216, 128), F32),
            pltpu.VMEM((4, 512, 256), BF16),
            pltpu.VMEM((4, 576, 1024), F32),
            pltpu.VMEM((18, 192, 512), BF16),
            pltpu.VMEM((1, 128), F32),
            pltpu.VMEM((1, 128), F32),
            pltpu.SemaphoreType.DMA((2,)),
        ],
        mib=24,
    )(
        row,
        raw,
        w4,
        in_hbm(stem_gain.reshape(1, -1)),
        in_hbm(stem_shift.reshape(1, -1)),
        taps,
    )
    others = [
        lax.ppermute(stat, "row", [(i, (i + by) % 4) for i in range(4)]) for by in (1, 2, 3)
    ]
    dw_bias = (down_weight, down_bias.reshape(1, -1))
    part = sds((128, 256), BF16)
    room = [pltpu.VMEM((128, 1024), BF16)]
    parts = {}

    def send(by):
        return lax.ppermute(parts[by], "tm", [(i, (i + by) % 4) for i in range(4)])

    parts[3], affine = call(
        functools.partial(first_kernel, 3),
        (part, sds((2, 256), F32)),
        [SMEM] + [VMEM] * 9,
        room,
    )(
        me,
        mix,
        stat,
        *others,
        mixer_gain.reshape(1, -1),
        mixer_shift.reshape(1, -1),
        *dw_bias,
    )
    parts[3] = send(3)
    for by in (2, 1, 0):
        parts[by] = call(
            functools.partial(next_kernel, by), part, [SMEM] + [VMEM] * 4, room
        )(me, mix, affine, *dw_bias)
        if by:
            parts[by] = send(by)
    placed = pl.pallas_call(
        place_kernel,
        out_shape=pltpu.HBM((4, 128, 256), BF16),
        in_specs=[SMEM] + [VMEM] * 4,
        out_specs=HBM,
        scratch_shapes=[pltpu.SemaphoreType.DMA((4,))],
        compiler_params=pltpu.CompilerParams(vmem_limit_bytes=1 << 20),
    )(me, *(parts[by] for by in range(4)))
    return placed.reshape(4, 2, 2, 32, 256)


def solution(mesh):
    return jax.shard_map(
        local,
        mesh=mesh,
        in_specs=(P("clip", None, "tm", "row"), P("clip")) + (P(),) * 9,
        out_specs=P("clip", "tm", "row", None, None),
        check_vma=False,
    )
```
